32 devices in a mesh: groups: 2 (over y), tile: 8 (over z, x), sub: 2 (over core).
Axes of the slice: x: 2, y: 2, z: 4, core: 2. Of those that a mesh axis runs over, the one named last changes fastest.
Arguments:
- features: bfloat16 [512, 128], P(('groups', 'tile')), parts along dimension 0, may hold values from -6 to 6
- weight: bfloat16 [3, 3, 48, 128], replicated, may hold values from -0.1875 to 0.1875
- out_bias: float32 [48], replicated, may hold values from -0.5 to 0.5
- band_tiles: int32 [32], P(('groups', 'tile')), parts along dimension 0, may hold values from 0 to 15, as said below
- band_width: int32 [4], P('groups'), parts along dimension 0, may hold values from 4 to 8, as said below
- cotangent: bfloat16 [32, 48, 128, 128], P(('groups', 'tile'), None, 'sub'), parts along dimension 0, may hold values from -0.29882812 to 0.29882812
Outputs:
- prediction: bfloat16 [32, 48, 128, 128], P(('groups', 'tile'), None, 'sub'), parts along dimension 0
- feature_grad: float32 [512, 128], P(('groups', 'tile')), parts along dimension 0
- weight_grad: float32 [6, 3, 48, 128], P('groups'), parts along dimension 0
- bias_grad: float32 [96], P('groups'), parts along dimension 0
The draws below stay inside these ranges and needn't reach their ends.
There are 2 independent parts, one for each index of `groups`. The reference program is written for one: setup_inputs(seed, part) draws one part's arguments, and reference() takes and returns one part's arrays. A program takes and returns all parts, laid end to end along the dimension named above; an argument that names none is the same for every part. Nothing has to cross between parts.
Inputs may be any that keep to these rules, and one draw needn't show every extreme that they name: `band_tiles`: each band tile number appears in exactly one slot; number t is tile row t // 8 at tile offset t % 8 from the diagonal. `band_width`: some tile row has width 8.
All inputs are finite; a program needn't handle non-finite values.
Results may differ from the reference program's by a relative error of at most 0.0048.
Values may be sent and summed in bfloat16 or wider, within the bound.
A program may use at most 128 MiB of HBM per device.

```python
import jax
import jax.numpy as jnp
from jax import lax

C = 128
CO = 48
RATE = 8
TILE = 128
BAND_T = 8
TPD = 2
SLOTS = 16
NB = 2
BINS = 256


def band_layout(key):
    base_key = jax.random.fold_in(key, 29)
    width_key, widest_key, tile_key, slot_key = jax.random.split(base_key, 4)
    widths = jax.random.randint(width_key, (NB,), BAND_T // 2, BAND_T + 1)
    widest = jax.random.randint(widest_key, (), 0, NB)
    widths = jnp.where(jnp.arange(NB) == widest, BAND_T, widths).astype(jnp.int32)
    tiles = jnp.arange(SLOTS, dtype=jnp.int32)
    usable = tiles % BAND_T < widths[tiles // BAND_T]
    tile_rank = jax.random.permutation(tile_key, SLOTS).astype(jnp.int32)
    tile_keys = jnp.where(usable, 0, SLOTS) + tile_rank
    tile_order = jnp.argsort(tile_keys, stable=True).astype(jnp.int32)
    slot_rank = jax.random.permutation(slot_key, SLOTS).astype(jnp.int32)
    slot_keys = jnp.where(tiles % TPD == 0, 0, SLOTS) + slot_rank
    slot_order = jnp.argsort(slot_keys, stable=True).astype(jnp.int32)
    placed = jnp.zeros((SLOTS,), jnp.int32).at[slot_order].set(tile_order)
    return (widths, placed)


def draw_band_width(key, part):
    return band_layout(key)[0]


def draw_band_tiles(key, part):
    return band_layout(key)[1]


def steps_of(key, dims, cuts, low, high):
    level, own = 1.0, jax.random.fold_in(key, 6)
    for axis_at, shards_of in cuts:
        heights = jnp.exp(jax.random.uniform(jax.random.fold_in(own, axis_at), (shards_of,), jnp.float32, low / len(cuts), high / len(cuts)))
        level = level * jnp.repeat(heights, dims[axis_at] // shards_of).reshape([-1 if axis == axis_at else 1 for axis in range(len(dims))])
    return level


def gaussian(rng, shape, width, bound, pieces=(), kind=jnp.bfloat16):
    loudness = steps_of(rng, shape, pieces, -0.22, 0.18) if pieces else 1.0
    drawn = jax.random.normal(rng, shape, jnp.float32) * width * loudness
    return jnp.minimum(jnp.maximum(drawn, -bound), bound).astype(kind)


def setup_inputs(seed: int = 0, part: int = 0) -> dict:
    seeds = jax.random.split(jax.random.key(seed), 7)
    part_splits = jax.random.split(jax.random.fold_in(seeds[6], part), 7)
    features = gaussian(part_splits[0], (BINS, C), 1.0, 6.0, ((0, 8),))
    weight = gaussian(seeds[1], (3, 3, CO, C), (9 * C) ** -0.5, 0.1875)
    out_bias = jnp.clip(jax.random.uniform(seeds[2], (CO,), jnp.float32, -0.5, 0.5), -0.5, 0.5)
    band_tiles = draw_band_tiles(jax.random.fold_in(jax.random.fold_in(seeds[6], part), 71), part)
    band_width = draw_band_width(jax.random.fold_in(jax.random.fold_in(seeds[6], part), 71), part)
    cotangent = gaussian(part_splits[5], (SLOTS, CO, TILE, TILE), 0.05, 0.29882812, ((0, 8), (2, 2)))
    return {"features": features, "weight": weight, "out_bias": out_bias, "band_tiles": band_tiles, "band_width": band_width, "cotangent": cotangent}


HIGHEST = lax.Precision.HIGHEST


def inside_bins(start_index, length, total_bins):
    positions = start_index - RATE + jnp.arange(length, dtype=jnp.int32)
    return (positions >= 0) & (positions < total_bins)


def add_rows(totals, piece, start_index):
    current = lax.dynamic_slice_in_dim(totals, start_index, piece.shape[0], 0)
    return lax.dynamic_update_slice_in_dim(totals, current + piece, start_index, 0)


def tile_terms(padded, weight, out_bias, grad_tile, row_start, col_start, total_bins):
    tile_rows = grad_tile.shape[1]
    tile_cols = grad_tile.shape[2]
    row_feat = lax.dynamic_slice_in_dim(padded, row_start, tile_rows + 2 * RATE, 0).astype(jnp.float32)
    col_feat = lax.dynamic_slice_in_dim(padded, col_start, tile_cols + 2 * RATE, 0).astype(jnp.float32)
    pair_sum = row_feat.T[:, :, None] + col_feat.T[:, None, :]
    rows_inside = inside_bins(row_start, tile_rows + 2 * RATE, total_bins)
    cols_inside = inside_bins(col_start, tile_cols + 2 * RATE, total_bins)
    active = (pair_sum > 0.0) & rows_inside[None, :, None] & cols_inside[None, None, :]
    hidden_low = lax.optimization_barrier(jnp.where(active, pair_sum, 0.0).astype(jnp.bfloat16))
    hidden = hidden_low.astype(jnp.float32)
    weight_full = weight.astype(jnp.float32)
    grad_full = grad_tile.astype(jnp.float32)
    grad_padded = jnp.pad(grad_full, ((0, 0), (2 * RATE, 2 * RATE), (2 * RATE, 2 * RATE)))
    predicted = jnp.zeros((grad_tile.shape[0], tile_rows, tile_cols), jnp.float32) + out_bias[:, None, None]
    hidden_grad = jnp.zeros(hidden.shape, jnp.float32)
    weight_rows = []
    for tap_row in range(3):
        tap_terms = []
        for tap_col in range(3):
            window = hidden[:, RATE * tap_row:RATE * tap_row + tile_rows, RATE * tap_col:RATE * tap_col + tile_cols]
            predicted = predicted + jnp.einsum("oc,cpq->opq", weight_full[tap_row, tap_col], window, precision=HIGHEST)
            tap_terms.append(jnp.einsum("cpq,opq->oc", window, grad_full, precision=HIGHEST))
            row_from = RATE * (2 - tap_row)
            col_from = RATE * (2 - tap_col)
            shifted = grad_padded[:, row_from:row_from + tile_rows + 2 * RATE, col_from:col_from + tile_cols + 2 * RATE]
            hidden_grad = hidden_grad + jnp.einsum("oc,opq->cpq", weight_full[tap_row, tap_col], shifted, precision=HIGHEST)
        weight_rows.append(jnp.stack(tap_terms))
    pair_grad = jnp.where(active, hidden_grad, 0.0)
    return (predicted.astype(jnp.bfloat16), jnp.sum(pair_grad, axis=2).T, jnp.sum(pair_grad, axis=1).T,
            jnp.stack(weight_rows), jnp.sum(grad_full, axis=(1, 2)))


def reference(features, weight, out_bias, band_tiles, band_width, cotangent):
    total_bins = features.shape[0]
    tail_bins = BAND_T * TILE
    padded = jnp.pad(features, ((RATE, RATE + tail_bins), (0, 0)))

    def one_slot(carried, inputs):
        tile_id, grad_tile = inputs
        tile_row = tile_id // BAND_T
        offset = tile_id % BAND_T
        is_valid = offset < band_width[tile_row]
        row_start = (tile_row * TILE).astype(jnp.int32)
        col_start = ((tile_row + offset) * TILE).astype(jnp.int32)

        def compute(held):
            rows_total, weight_total, bias_total = held
            predicted, row_part, col_part, weight_part, bias_part = tile_terms(
                padded, weight, out_bias, grad_tile, row_start, col_start, total_bins)
            rows_total = add_rows(rows_total, row_part, row_start)
            rows_total = add_rows(rows_total, col_part, col_start)
            return predicted, rows_total, weight_total + weight_part, bias_total + bias_part

        def skipped(held):
            return (jnp.zeros(grad_tile.shape, jnp.bfloat16), held[0], held[1], held[2])

        predicted, rows_total, weight_total, bias_total = lax.cond(is_valid, compute, skipped, carried)
        return (rows_total, weight_total, bias_total), predicted

    start_state = (jnp.zeros((total_bins + 2 * RATE + tail_bins, features.shape[1]), jnp.float32),
                   jnp.zeros(weight.shape, jnp.float32), jnp.zeros(out_bias.shape, jnp.float32))
    final_state, prediction = lax.scan(one_slot, start_state, (band_tiles, cotangent))
    rows_total, weight_total, bias_total = final_state
    return (prediction, rows_total[RATE:RATE + total_bins], weight_total, bias_total)
```

```python
import functools

import jax
import jax.numpy as jnp
from jax import lax
from jax.experimental import pallas as pl
from jax.experimental.pallas import tpu as pltpu
from jax.sharding import PartitionSpec as P

RATE = 8
TILE = 128
BAND_T = 8
WIDE = TILE + 2 * RATE
PAIR = 2 * RATE
LANES = 128
HALF = 64
FAR = -1e30
MESH = pl.DeviceIdType.MESH
F32 = jnp.float32
BF16 = jnp.bfloat16


def prep_kernel(
    tiles, x_hbm, cot_hbm, weight_hbm, bias_hbm, ids_hbm, width_hbm,
    feat_ref, hgrad_ref, cotp_ref, weight_k_ref, bias_ref, out_bias_ref, ids_ref, width_ref,
    held, cots, weights, stacked, flat, even, odd,
    send_sem, recv_sem, own_sem, cot_sem, weight_sem, table_sem,
):
    me = lax.axis_index("tile")
    rows = x_hbm.shape[0]
    total = tiles * rows
    slots, out_channels, sub_rows, _ = cots.shape
    blocks = (sub_rows + PAIR) // PAIR

    def peer_of(d):
        return lax.rem(me + d, tiles)

    barrier = pltpu.get_barrier_semaphore()

    def greet(d, carry):
        pl.semaphore_signal(barrier, inc=1, device_id={"tile": peer_of(d)}, device_id_type=MESH)
        return carry

    lax.fori_loop(1, tiles, greet, 0)

    own = pltpu.make_async_copy(x_hbm, held.at[me], own_sem)
    own.start()
    weight_copy = pltpu.make_async_copy(weight_hbm, weights, weight_sem)
    weight_copy.start()

    def cot_copy(slot):
        return pltpu.make_async_copy(cot_hbm.at[slot], cots.at[slot], cot_sem.at[slot])

    for slot in range(slots):
        cot_copy(slot).start()
    tables = [
        pltpu.make_async_copy(source, target, table_sem.at[at])
        for at, (source, target) in enumerate(
            ((bias_hbm, out_bias_ref), (ids_hbm, ids_ref), (width_hbm, width_ref))
        )
    ]
    for table in tables:
        table.start()

    feat_ref[0:RATE, :] = jnp.full((RATE, LANES), FAR, F32)
    tail = feat_ref.shape[0] - RATE - total
    feat_ref[RATE + total :, :] = jnp.full((tail, LANES), FAR, F32)
    for slab in (0, blocks):
        even[slab] = jnp.zeros(even.shape[1:], BF16)
        odd[slab] = jnp.zeros(odd.shape[1:], BF16)
    edge = jnp.zeros((blocks - 1, RATE, PAIR, LANES), BF16)
    even[1:blocks, :, 0:PAIR] = edge
    even[1:blocks, :, PAIR + TILE :] = edge
    stacked[...] = jnp.zeros_like(stacked)
    for slot in range(slots):
        cotp_ref[slot, 0:PAIR] = jnp.zeros((PAIR, out_channels, TILE), BF16)
        cotp_ref[slot, PAIR + sub_rows :] = jnp.zeros((PAIR, out_channels, TILE), BF16)
    weight_copy.wait()
    for j in range(4):
        for r in range(2):
            a = r + j - 1
            if 0 <= a <= 2:
                for b in range(3):
                    at = (b * 4 + j) * HALF
                    stacked[at : at + out_channels, r * LANES : (r + 1) * LANES] = weights[a, b]
    for b in range(3):
        for r in range(2):
            at = (r * 3 + b) * LANES
            weight_k_ref[at : at + LANES, :] = jnp.transpose(
                stacked[b * 4 * HALF : (b + 1) * 4 * HALF, r * LANES : (r + 1) * LANES], (1, 0)
            )

    def arrange(slot):
        cot_copy(slot).wait()
        sums = []
        for o in range(out_channels):
            block = cots[slot, o].astype(F32)
            flat[o * sub_rows : (o + 1) * sub_rows, :] = block
            sums.append(jnp.sum(block, axis=0, keepdims=True))
        column = jnp.sum(jnp.transpose(jnp.concatenate(sums, axis=0), (1, 0)), axis=0, keepdims=True)
        bias_ref[slot] = jnp.zeros((RATE, LANES), F32)
        bias_ref[slot, 0:1, 0:out_channels] = column

        @pl.loop(0, sub_rows, unroll=16)
        def _(p):
            cotp_ref[slot, PAIR + p] = flat[pl.ds(p, out_channels, stride=sub_rows), :].astype(BF16)

    def turn(slot):
        @pl.loop(0, blocks - 1)
        def _(k):
            low = jnp.zeros((HALF - out_channels, TILE), BF16)
            rim = jnp.zeros((RATE, LANES), F32)
            for i in range(RATE):
                at = PAIR + k * PAIR + i
                both = jnp.concatenate([cotp_ref[slot, at + RATE], low, cotp_ref[slot, at], low], axis=0)
                turned = jnp.transpose(both, (1, 0))
                even[k + 1, i, PAIR : PAIR + TILE] = turned
                odd[k + 1, i] = jnp.concatenate([rim, turned.astype(F32), rim], axis=0).astype(BF16)

    def backward(slot):
        @pl.loop(0, blocks)
        def _(k):
            left = jnp.concatenate(
                [
                    jnp.concatenate(
                        [
                            even[k + 1, i, PAIR:], even[k, i, PAIR:],
                            odd[k + 1, i], odd[k, i],
                            even[k + 1, i, 0:WIDE], even[k, i, 0:WIDE],
                        ],
                        axis=1,
                    )
                    for i in range(RATE)
                ],
                axis=0,
            )
            back = jnp.dot(left, stacked[...], preferred_element_type=F32)
            for i in range(RATE):
                for r in range(2):
                    p = k * PAIR + r * RATE + i
                    hgrad_ref[slot, p] = back[i * WIDE : (i + 1) * WIDE, r * LANES : (r + 1) * LANES]

    arrange(0)
    own.wait()
    pl.semaphore_wait(barrier, tiles - 1)

    def copy_of(d):
        return pltpu.make_async_remote_copy(
            src_ref=held.at[me],
            dst_ref=held.at[me],
            send_sem=send_sem.at[d],
            recv_sem=recv_sem.at[d],
            device_id={"tile": peer_of(d)},
            device_id_type=MESH,
        )

    def start(d, carry):
        copy_of(d).start()
        return carry

    lax.fori_loop(1, tiles, start, 0)
    mine = pl.multiple_of(RATE + me * rows, RATE)
    feat_ref[pl.ds(mine, rows), :] = held[me].astype(F32)
    turn(0)
    backward(0)
    for slot in range(1, slots):
        arrange(slot)
        turn(slot)
        backward(slot)
    for table in tables:
        table.wait()

    def finish(d, carry):
        copy_of(d).wait()
        source = lax.rem(me - d + tiles, tiles)
        at = pl.multiple_of(RATE + source * rows, RATE)
        feat_ref[pl.ds(at, rows), :] = held[source].astype(F32)
        return carry

    lax.fori_loop(1, tiles, finish, 0)


def compute_kernel(
    sub_rows, tiles, rows, chunk_rows, total_bins,
    ids_in, width_in, feat_ref, hgrad_ref, cotp_ref, weight_k_ref, bias_ref, out_bias_ref,
    pred_hbm, send_ref,
    ids_ref, width_ref, stage, lined, kept, bias_row, col_acc, row_acc, weight_acc, feat_acc, bias_acc,
    pred_sem, table_sem,
):
    ids_copy = pltpu.make_async_copy(ids_in, ids_ref, table_sem.at[0])
    width_copy = pltpu.make_async_copy(width_in, width_ref, table_sem.at[1])
    ids_copy.start()
    width_copy.start()
    slots, _, out_channels, _ = cotp_ref.shape
    sub = lax.axis_index("sub")
    ext = sub_rows + PAIR
    blocks = ext // PAIR

    weight_acc[...] = jnp.zeros_like(weight_acc)
    feat_acc[...] = jnp.zeros_like(feat_acc)
    bias_acc[...] = jnp.zeros_like(bias_acc)
    bias_row[...] = jnp.zeros_like(bias_row)
    bias_row[0:1, 0:out_channels] = out_bias_ref[...]
    bias_row[0:1, HALF : HALF + out_channels] = out_bias_ref[...]

    ids_copy.wait()
    width_copy.wait()

    def write_of(slot):
        return pltpu.make_async_copy(
            stage.at[slot, :, pl.ds(PAIR, sub_rows), :], pred_hbm.at[slot], pred_sem.at[slot]
        )

    @pl.loop(0, slots)
    def _(slot):
        tile_id = ids_ref[slot]
        tile_row = tile_id // BAND_T
        offset = tile_id - tile_row * BAND_T
        valid = offset < width_ref[tile_row]
        row_start = pl.multiple_of(tile_row * TILE + sub * sub_rows, RATE)
        col_start = pl.multiple_of((tile_row + offset) * TILE, TILE)
        reaches = jnp.logical_and(valid, col_start <= total_bins)

        @pl.when(jnp.logical_not(valid))
        def _():
            stage[slot] = jnp.zeros(stage.shape[1:], BF16)

        @pl.when(valid)
        def _():
            bias_acc[...] += bias_ref[slot]

        @pl.when(jnp.logical_and(valid, jnp.logical_not(reaches)))
        def _():
            wide = jnp.transpose(jnp.broadcast_to(bias_row[0:1, :], (TILE, LANES)), (1, 0))
            filled = jnp.broadcast_to(wide[0:out_channels][:, None, :], (out_channels, PAIR, TILE)).astype(BF16)
            for k in range(1, blocks):
                stage[slot, :, k * PAIR : (k + 1) * PAIR, :] = filled

        def sweep(k, columns):
            first = k * PAIR
            span = WIDE if columns == 3 else RATE
            col_full = feat_ref[pl.ds(col_start, span), :]
            if columns == 3:
                even_col = feat_ref[pl.ds(col_start, WIDE), :].astype(BF16).reshape(WIDE // PAIR, PAIR, LANES)
                odd_col = feat_ref[pl.ds(col_start + RATE, TILE), :].astype(BF16).reshape(TILE // PAIR, PAIR, LANES)
            else:
                even_col = feat_ref[pl.ds(col_start, TILE), :].astype(BF16).reshape(TILE // PAIR, PAIR, LANES)
            zero = jnp.zeros((), BF16)
            hidden = []
            for i in range(RATE):
                taps = []
                for r in range(2):
                    row = feat_ref[pl.ds(row_start + first + r * RATE + i, 1), :]
                    wide = jnp.broadcast_to(row, (PAIR, LANES)).astype(BF16)[None]
                    even = jnp.maximum(even_col + wide, zero)
                    if columns == 3:
                        even = even.reshape(WIDE, LANES)
                        odd = jnp.maximum(odd_col + wide, zero).reshape(TILE, LANES)
                        taps += [even[0:TILE], odd, even[PAIR:WIDE]]
                    else:
                        taps += [even.reshape(TILE, LANES)]
                hidden.append(jnp.concatenate(taps, axis=1))
            hidden = jnp.concatenate(hidden, axis=0)
            cot = jnp.concatenate(
                [
                    jnp.concatenate(
                        [cotp_ref[slot, PAIR + first + i + RATE * (1 - j)] for j in range(4)], axis=0
                    )
                    for i in range(RATE)
                ],
                axis=1,
            )
            product = jnp.dot(cot, hidden, preferred_element_type=F32)
            if columns == 3:
                weight_acc[...] += product
                weights = weight_k_ref[...]
            else:
                weight_acc[:, 0:LANES] += product[:, 0:LANES]
                weight_acc[:, 3 * LANES : 4 * LANES] += product[:, LANES:]
                weights = jnp.concatenate(
                    [weight_k_ref[0:LANES, :], weight_k_ref[3 * LANES : 4 * LANES, :]], axis=0
                )
            ahead = jnp.dot(hidden, weights, preferred_element_type=F32)
            for i in range(RATE):
                here = ahead[i * TILE : (i + 1) * TILE, LANES:] + kept[i * TILE : (i + 1) * TILE, :]
                here = (here + bias_row[0:1, :]).astype(BF16)
                turned = jnp.transpose(here, (1, 0)).astype(F32)
                lined[(RATE + i) * out_channels : (RATE + i + 1) * out_channels, :] = turned[0:out_channels]
                lined[i * out_channels : (i + 1) * out_channels, :] = turned[HALF : HALF + out_channels]
            kept[...] = ahead[:, 0:LANES]
            at = pl.multiple_of(k * PAIR, PAIR)
            for o in range(out_channels):
                stage[slot, o, pl.ds(at, PAIR), :] = lined[pl.ds(o, PAIR, stride=out_channels), :].astype(BF16)
            gathered = jnp.zeros((span, LANES), F32)
            for p in range(PAIR):
                row = feat_ref[pl.ds(row_start + first + p, 1), :]
                full = jnp.where(col_full + row > 0.0, hgrad_ref[slot, first + p, 0:span], 0.0)
                gathered = gathered + full
                row_acc[pl.ds(first + p, 1), :] = jnp.sum(full, axis=0, keepdims=True)
            col_acc[0:span] += gathered

        @pl.when(reaches)
        def _():
            col_acc[...] = jnp.zeros_like(col_acc)

            @pl.when(col_start < total_bins)
            def _():
                pl.loop(0, blocks)(lambda k: sweep(k, 3))

            @pl.when(col_start >= total_bins)
            def _():
                pl.loop(0, blocks)(lambda k: sweep(k, 1))

            feat_acc[pl.ds(row_start, ext), :] += row_acc[...]
            feat_acc[pl.ds(col_start, WIDE), :] += col_acc[...]

        write_of(slot).start()

    granules = []
    for a in range(3):
        for b in range(3):
            full = (
                weight_acc[(a + 1) * out_channels : (a + 2) * out_channels, b * LANES : (b + 1) * LANES]
                + weight_acc[a * out_channels : (a + 1) * out_channels, (3 + b) * LANES : (4 + b) * LANES]
            ).astype(BF16)
            for at in range(0, out_channels, 16):
                granules.append(full[at : at + 16])
    granules.append(jnp.concatenate([bias_acc[...], jnp.zeros_like(bias_acc)], axis=0).astype(BF16))
    per = chunk_rows // 16
    for g, value in enumerate(granules):
        owner, at = g // per, rows + (g % per) * 16
        send_ref[owner // 2, owner % 2, at : at + 16, :] = value
    used = len(granules) // per
    for g in range(len(granules), -(-len(granules) // per) * per):
        owner, at = g // per, rows + (g % per) * 16
        send_ref[owner // 2, owner % 2, at : at + 16, :] = jnp.zeros((16, LANES), BF16)

    def rest(e, carry):
        send_ref[e // 2, e % 2, rows:, :] = jnp.zeros((chunk_rows, LANES), BF16)
        return carry

    lax.fori_loop(-(-len(granules) // per), 2 * tiles, rest, 0)

    @pl.loop(0, tiles)
    def _(t):
        start = pl.multiple_of(RATE + t * rows, RATE)
        value = feat_acc[pl.ds(start, rows), :].astype(BF16)
        for half in range(2):
            send_ref[t, half, 0:rows, :] = value

    @pl.loop(0, slots)
    def _(slot):
        write_of(slot).wait()


def reduce_kernel(tiles, rows, send_ref, feat_ref, all_ref, arrived, scatter_sem, gather_sem):
    me = lax.axis_index("tile")
    sub = lax.axis_index("sub")
    mine = me * 2 + sub
    count = 2 * tiles

    def peer_of(d):
        return lax.rem(mine + d, count)

    def place(e):
        return {"tile": e // 2, "sub": lax.rem(e, 2)}

    barrier = pltpu.get_barrier_semaphore()

    def greet(d, carry):
        pl.semaphore_signal(barrier, inc=1, device_id=place(peer_of(d)), device_id_type=MESH)
        return carry

    lax.fori_loop(1, count, greet, 0)
    arrived[me, sub] = send_ref[me, sub]
    pl.semaphore_wait(barrier, count - 1)

    def scatter_of(d):
        e = peer_of(d)
        return pltpu.make_async_remote_copy(
            src_ref=send_ref.at[e // 2, lax.rem(e, 2)], dst_ref=arrived.at[me, sub],
            send_sem=scatter_sem.at[0, d], recv_sem=scatter_sem.at[1, d],
            device_id=place(e), device_id_type=MESH,
        )

    def gather_of(d):
        return pltpu.make_async_remote_copy(
            src_ref=all_ref.at[me, sub], dst_ref=all_ref.at[me, sub],
            send_sem=gather_sem.at[0, d], recv_sem=gather_sem.at[1, d],
            device_id=place(peer_of(d)), device_id_type=MESH,
        )

    def run(step):
        def body(d, carry):
            step(d)
            return carry

        lax.fori_loop(1, count, body, 0)

    run(lambda d: scatter_of(d).start())
    run(lambda d: scatter_of(d).wait())

    def add(t, total):
        return total + arrived[t, 0].astype(F32) + arrived[t, 1].astype(F32)

    total = lax.fori_loop(0, tiles, add, jnp.zeros(arrived.shape[2:], F32))
    all_ref[me, sub] = total[rows:].astype(BF16)
    run(lambda d: gather_of(d).start())
    feat_ref[...] = total[0:rows]
    run(lambda d: gather_of(d).wait())


def finish_kernel(weight_rows, feat_in, sums_in, feat_ref, weight_ref, bias_ref):
    feat_ref[...] = feat_in[...]
    sums = sums_in[...].astype(F32).reshape(-1, LANES)
    weight_ref[...] = sums[:weight_rows]
    bias_ref[...] = sums[weight_rows : weight_rows + 1, 0 : bias_ref.shape[1]]


def on_device(tiles, features, weight, out_bias, band_tiles, band_width, cotangent):
    rows, channels = features.shape
    slots, out_channels, sub_rows, _ = cotangent.shape
    total_bins = tiles * rows
    ext = sub_rows + PAIR
    blocks = ext // PAIR
    padded_rows = total_bins + WIDE
    weight_rows = 9 * out_channels
    chunk_rows = -(-(weight_rows + 16) // (2 * tiles * 16)) * 16
    vmem = pl.BlockSpec(memory_space=pltpu.VMEM)
    hbm = pl.BlockSpec(memory_space=pltpu.HBM)
    dma = pltpu.SemaphoreType.DMA
    shape = jax.ShapeDtypeStruct

    padded, hgrad, cotp, weight_k, bias, bias_in, ids, width = pl.pallas_call(
        functools.partial(prep_kernel, tiles),
        out_shape=(
            shape((padded_rows, channels), F32),
            shape((slots, ext, WIDE, channels), F32),
            shape((slots, ext + PAIR, out_channels, TILE), BF16),
            shape((6 * channels, 4 * HALF), BF16),
            shape((slots, RATE, LANES), F32),
            shape((1, out_channels), F32),
            shape(band_tiles.shape, band_tiles.dtype),
            shape(band_width.shape, band_width.dtype),
        ),
        in_specs=[hbm] * 6,
        out_specs=(vmem,) * 8,
        scratch_shapes=[
            pltpu.VMEM((tiles, rows, channels), BF16),
            pltpu.VMEM(cotangent.shape, BF16),
            pltpu.VMEM(weight.shape, BF16),
            pltpu.VMEM((12 * HALF, 2 * channels), BF16),
            pltpu.VMEM((out_channels * sub_rows, TILE), F32),
            pltpu.VMEM((blocks + 1, RATE, WIDE + PAIR, LANES), BF16),
            pltpu.VMEM((blocks + 1, RATE, WIDE, LANES), BF16),
            dma((tiles,)),
            dma((tiles,)),
            dma,
            dma((slots,)),
            dma,
            dma((3,)),
        ],
        compiler_params=pltpu.CompilerParams(
            collective_id=0, has_side_effects=True, vmem_limit_bytes=36 << 20
        ),
    )(
        *(
            pltpu.with_memory_space_constraint(x, pltpu.HBM)
            for x in (
                features, cotangent, weight, out_bias.reshape(1, out_channels), band_tiles, band_width
            )
        )
    )

    prediction, parts = pl.pallas_call(
        functools.partial(compute_kernel, sub_rows, tiles, rows, chunk_rows, total_bins),
        out_shape=(
            shape(cotangent.shape, BF16),
            shape((tiles, 2, rows + chunk_rows, channels), BF16),
        ),
        in_specs=[vmem] * 8,
        out_specs=(hbm, vmem),
        scratch_shapes=[
            pltpu.SMEM(band_tiles.shape, band_tiles.dtype),
            pltpu.SMEM(band_width.shape, band_width.dtype),
            pltpu.VMEM((slots, out_channels, ext, TILE), BF16),
            pltpu.VMEM((PAIR * out_channels, TILE), F32),
            pltpu.VMEM((RATE * TILE, LANES), F32),
            pltpu.VMEM((RATE, LANES), F32),
            pltpu.VMEM((WIDE, channels), F32),
            pltpu.VMEM((ext, channels), F32),
            pltpu.VMEM((4 * out_channels, 6 * channels), F32),
            pltpu.VMEM((padded_rows, channels), F32),
            pltpu.VMEM((RATE, LANES), F32),
            dma((slots,)),
            dma((2,)),
        ],
        compiler_params=pltpu.CompilerParams(vmem_limit_bytes=36 << 20),
    )(
        ids, width, padded, hgrad, cotp, weight_k, bias, bias_in,
    )

    feature_grad, sums = pl.pallas_call(
        functools.partial(reduce_kernel, tiles, rows),
        out_shape=(
            shape((rows, channels), F32),
            shape((tiles, 2, chunk_rows, channels), BF16),
        ),
        in_specs=[vmem],
        out_specs=(vmem, vmem),
        scratch_shapes=[
            pltpu.VMEM((tiles, 2, rows + chunk_rows, channels), BF16),
            dma((2, 2 * tiles)),
            dma((2, 2 * tiles)),
        ],
        compiler_params=pltpu.CompilerParams(
            collective_id=1, has_side_effects=True, vmem_limit_bytes=32 << 20
        ),
    )(parts)
    feature_grad, weight_grad, bias_grad = pl.pallas_call(
        functools.partial(finish_kernel, weight_rows),
        out_shape=(
            shape((rows, channels), F32),
            shape((weight_rows, channels), F32),
            shape((1, out_channels), F32),
        ),
        in_specs=[vmem, vmem],
        out_specs=(vmem, vmem, vmem),
        compiler_params=pltpu.CompilerParams(vmem_limit_bytes=32 << 20),
    )(feature_grad, sums)
    return (
        prediction,
        feature_grad,
        weight_grad.reshape(weight.shape),
        bias_grad.reshape(out_channels),
    )


def solution(mesh):
    in_specs = (
        P(("groups", "tile"), None),
        P(),
        P(),
        P(("groups", "tile")),
        P("groups"),
        P(("groups", "tile"), None, "sub", None),
    )
    out_specs = (
        P(("groups", "tile"), None, "sub", None),
        P(("groups", "tile"), None),
        P("groups", None, None, None),
        P("groups"),
    )
    return jax.shard_map(
        functools.partial(on_device, mesh.shape["tile"]),
        mesh=mesh, in_specs=in_specs, out_specs=out_specs, check_vma=False,
    )
```

```python
import functools

import jax
import jax.numpy as jnp
from jax import lax
from jax.experimental import pallas as pl
from jax.experimental.pallas import tpu as pltpu
from jax.sharding import PartitionSpec as P

RATE = 8
TILE = 128
BAND_T = 8
WIDE = TILE + 2 * RATE
PAIR = 2 * RATE
LANES = 128
HALF = 64
FAR = -1e30
MESH = pl.DeviceIdType.MESH
F32 = jnp.float32
BF16 = jnp.bfloat16


def place_of(e):
    return {"tile": e // 2, "sub": lax.rem(e, 2)}


def fused_kernel(
    tiles, x_hbm, cot_hbm, weight_hbm, bias_hbm, ids_hbm, width_hbm,
    stage, feat_out, sums_out,
    ids_ref, width_ref, out_bias_ref, held, feat_ref, cots, weights, stacked, weight_k,
    flat, cotp, even, odd, hgrad, bias_ref, bias_rows,
    col_even, col_odd, col_full, row_full, hid_even, hid_odd, weight_acc,
    row_acc, col_acc, feat_acc, lined, kept,
    send_sums, arrived_sums, send_feat, arrived_feat,
    table_sem, cot_sem, gather_sem, scatter_sem, feat_sem, share_sem, pass_sem,
):
    me = lax.axis_index("tile")
    sub = lax.axis_index("sub")
    mine = me * 2 + sub
    count = 2 * tiles
    rows = x_hbm.shape[0]
    total = tiles * rows
    slots, out_channels, sub_rows, _ = cots.shape
    ext = sub_rows + PAIR
    blocks = ext // PAIR
    chunk_rows = send_sums.shape[2]
    half_rows = rows // 2

    def each(low, high, step):
        def body(d, carry):
            step(d)
            return carry

        lax.fori_loop(low, high, body, 0)

    def peer_of(d):
        return lax.rem(mine + d, count)

    def tile_of(d):
        return lax.rem(me + d, tiles)

    def remote(source, target, sems, d, where):
        return pltpu.make_async_remote_copy(
            src_ref=source, dst_ref=target, send_sem=sems.at[0, d], recv_sem=sems.at[1, d],
            device_id=where, device_id_type=MESH,
        )

    barrier = pltpu.get_barrier_semaphore()
    each(
        1, count,
        lambda d: pl.semaphore_signal(
            barrier, inc=1, device_id=place_of(peer_of(d)), device_id_type=MESH
        ),
    )

    local = [
        pltpu.make_async_copy(source, target, table_sem.at[at])
        for at, (source, target) in enumerate(
            (
                (x_hbm, held.at[me]), (weight_hbm, weights), (bias_hbm, out_bias_ref),
                (ids_hbm, ids_ref), (width_hbm, width_ref),
            )
        )
    ]
    for copy in local:
        copy.start()

    def cot_copy(slot):
        return pltpu.make_async_copy(cot_hbm.at[slot], cots.at[slot], cot_sem.at[slot])

    for slot in range(slots):
        cot_copy(slot).start()

    feat_ref[0:RATE, :] = jnp.full((RATE, LANES), FAR, F32)
    tail = feat_ref.shape[0] - RATE - total
    feat_ref[RATE + total :, :] = jnp.full((tail, LANES), FAR, F32)
    for slab in (0, blocks):
        even[slab] = jnp.zeros(even.shape[1:], BF16)
        odd[slab] = jnp.zeros(odd.shape[1:], BF16)
    edge = jnp.zeros((blocks - 1, RATE, PAIR, LANES), BF16)
    even[1:blocks, :, 0:PAIR] = edge
    even[1:blocks, :, PAIR + TILE :] = edge
    stacked[...] = jnp.zeros_like(stacked)
    weight_acc[...] = jnp.zeros_like(weight_acc)
    feat_acc[...] = jnp.zeros_like(feat_acc)
    col_acc[...] = jnp.zeros_like(col_acc)
    kept[...] = jnp.zeros_like(kept)
    bias_rows[...] = jnp.zeros_like(bias_rows)
    for slot in range(slots):
        cotp[slot, 0:PAIR] = jnp.zeros((PAIR, out_channels, TILE), BF16)
        cotp[slot, PAIR + sub_rows :] = jnp.zeros((PAIR, out_channels, TILE), BF16)
    for copy in local:
        copy.wait()
    for j in range(4):
        for r in range(2):
            a = r + j - 1
            if 0 <= a <= 2:
                for b in range(3):
                    at = (b * 4 + j) * HALF
                    stacked[at : at + out_channels, r * LANES : (r + 1) * LANES] = weights[a, b]
    for b in range(3):
        for r in range(2):
            at = (r * 3 + b) * LANES
            weight_k[at : at + LANES, :] = jnp.transpose(
                stacked[b * 4 * HALF : (b + 1) * 4 * HALF, r * LANES : (r + 1) * LANES], (1, 0)
            )

    bands = total // TILE
    valids, row_tiles, col_tiles = [], [], []
    for slot in range(slots):
        tile_id = ids_ref[slot]
        tile_row = tile_id // BAND_T

        def width_at(n, width, tile_row=tile_row):
            return jnp.where(tile_row == n, width_ref[n], width)

        width = lax.fori_loop(0, bands, width_at, jnp.int32(0))
        offset = tile_id - tile_row * BAND_T
        valids.append(offset < width)
        row_tiles.append(jnp.where(valids[slot], tile_row, -1))
        col_tiles.append(jnp.where(valids[slot], tile_row + offset, -1))
        value = jnp.where(valids[slot], out_bias_ref[...], 0.0)
        bias_rows[slot, 0:1, 0:out_channels] = value
        bias_rows[slot, 0:1, HALF : HALF + out_channels] = value

    def arrange(slot):
        cot_copy(slot).wait()
        sums = []
        for o in range(out_channels):
            block = cots[slot, o].astype(F32)
            flat[o * sub_rows : (o + 1) * sub_rows, :] = block
            sums.append(jnp.sum(block, axis=0, keepdims=True))
        column = jnp.sum(jnp.transpose(jnp.concatenate(sums, axis=0), (1, 0)), axis=0, keepdims=True)
        bias_ref[slot] = jnp.zeros((RATE, LANES), F32)
        bias_ref[slot, 0:1, 0:out_channels] = column

        @pl.loop(0, sub_rows, unroll=16)
        def _(p):
            cotp[slot, PAIR + p] = flat[pl.ds(p, out_channels, stride=sub_rows), :].astype(BF16)

    def turn(slot):
        @pl.loop(0, blocks - 1)
        def _(k):
            low = jnp.zeros((HALF - out_channels, TILE), BF16)
            rim = jnp.zeros((RATE, LANES), F32)
            for i in range(RATE):
                at = PAIR + k * PAIR + i
                both = jnp.concatenate([cotp[slot, at + RATE], low, cotp[slot, at], low], axis=0)
                turned = jnp.transpose(both, (1, 0))
                even[k + 1, i, PAIR : PAIR + TILE] = turned
                odd[k + 1, i] = jnp.concatenate([rim, turned.astype(F32), rim], axis=0).astype(BF16)

    def backward(slot):
        @pl.loop(0, blocks)
        def _(k):
            left = jnp.concatenate(
                [
                    jnp.concatenate(
                        [
                            even[k + 1, i, PAIR:], even[k, i, PAIR:],
                            odd[k + 1, i], odd[k, i],
                            even[k + 1, i, 0:WIDE], even[k, i, 0:WIDE],
                        ],
                        axis=1,
                    )
                    for i in range(RATE)
                ],
                axis=0,
            )
            back = jnp.dot(left, stacked[...], preferred_element_type=F32)
            for i in range(RATE):
                for r in range(2):
                    p = k * PAIR + r * RATE + i
                    hgrad[slot, p] = back[i * WIDE : (i + 1) * WIDE, r * LANES : (r + 1) * LANES]

    def gather_of(d):
        return remote(held.at[me], held.at[me], gather_sem, d, {"tile": tile_of(d)})

    arrange(0)
    pl.semaphore_wait(barrier, count - 1)
    each(1, tiles, lambda d: gather_of(d).start())
    at = pl.multiple_of(RATE + me * rows, RATE)
    feat_ref[pl.ds(at, rows), :] = held[me].astype(F32)
    for slot in range(1, slots):
        arrange(slot)
    turn(0)
    backward(0)

    def arrive(d):
        gather_of(d).wait()
        source = lax.rem(me - d + tiles, tiles)
        to = pl.multiple_of(RATE + source * rows, RATE)
        feat_ref[pl.ds(to, rows), :] = held[source].astype(F32)

    each(1, tiles, arrive)

    def row_at(n):
        return pl.multiple_of(n * TILE + sub * sub_rows, RATE)

    def col_at(n):
        return pl.multiple_of(n * TILE, TILE)

    for slot in range(slots):

        def take_row(n, held_rows, slot=slot):
            return jnp.where(row_tiles[slot] == n, feat_ref[pl.ds(row_at(n), ext), :], held_rows)

        def take_col(n, held_cols, slot=slot):
            return jnp.where(col_tiles[slot] == n, feat_ref[pl.ds(col_at(n), WIDE), :], held_cols)

        row_full[slot] = lax.fori_loop(0, bands, take_row, jnp.full((ext, LANES), FAR, F32))
        cols = lax.fori_loop(0, bands + 1, take_col, jnp.full((WIDE, LANES), FAR, F32))
        col_full[slot] = cols
        col_even[slot] = cols.astype(BF16)
        col_odd[slot] = cols[RATE : RATE + TILE].astype(BF16)

    @pl.loop(0, blocks)
    def _(k):
        zero = jnp.zeros((), BF16)
        right, left = [], []
        for slot in range(slots):
            base_even = col_even[slot].reshape(WIDE // PAIR, PAIR, LANES)
            base_odd = col_odd[slot].reshape(TILE // PAIR, PAIR, LANES)
            for i in range(RATE):
                taps = []
                for r in range(2):
                    p = k * PAIR + r * RATE + i
                    row = row_full[slot, pl.ds(p, 1), :]
                    wide = jnp.broadcast_to(row, (PAIR, LANES)).astype(BF16)[None]
                    pair_even = jnp.maximum(base_even + wide, zero).reshape(WIDE, LANES)
                    pair_odd = jnp.maximum(base_odd + wide, zero).reshape(TILE, LANES)
                    hid_even[slot, p] = pair_even
                    hid_odd[slot, p] = pair_odd
                    taps += [pair_even[0:TILE], pair_odd, pair_even[PAIR:WIDE]]
                right.append(jnp.concatenate(taps, axis=1))
                left.append(
                    jnp.concatenate(
                        [cotp[slot, PAIR + k * PAIR + i + RATE * (1 - j)] for j in range(4)], axis=0
                    )
                )
        weight_acc[...] += jnp.dot(
            jnp.concatenate(left, axis=1), jnp.concatenate(right, axis=0), preferred_element_type=F32
        )

    granules = []
    for a in range(3):
        for b in range(3):
            full = (
                weight_acc[(a + 1) * out_channels : (a + 2) * out_channels, b * LANES : (b + 1) * LANES]
                + weight_acc[a * out_channels : (a + 1) * out_channels, (3 + b) * LANES : (4 + b) * LANES]
            ).astype(BF16)
            for at in range(0, out_channels, 16):
                granules.append(full[at : at + 16])
    bias_sum = jnp.zeros((RATE, LANES), F32)
    for slot in range(slots):
        bias_sum = bias_sum + jnp.where(valids[slot], bias_ref[slot], 0.0)
    granules.append(jnp.concatenate([bias_sum, jnp.zeros_like(bias_sum)], axis=0).astype(BF16))
    per = chunk_rows // 16
    owners = -(-len(granules) // per)
    for g in range(owners * per):
        value = granules[g] if g < len(granules) else jnp.zeros((16, LANES), BF16)
        at = (g % per) * 16
        send_sums[g // per // 2, g // per % 2, at : at + 16, :] = value

    def rest(e):
        send_sums[e // 2, lax.rem(e, 2)] = jnp.zeros((chunk_rows, LANES), BF16)

    each(owners, count, rest)

    def scatter_of(d):
        e = peer_of(d)
        return remote(
            send_sums.at[e // 2, lax.rem(e, 2)], arrived_sums.at[me, sub], scatter_sem, d, place_of(e)
        )

    def share_of(d):
        return remote(
            sums_out.at[me, sub], sums_out.at[me, sub], share_sem, d, place_of(peer_of(d))
        )

    def feat_of(d):
        e = peer_of(d)
        return remote(
            send_feat.at[e // 2, lax.rem(e, 2)], arrived_feat.at[me, sub], feat_sem, d, place_of(e)
        )

    each(1, count, lambda d: scatter_of(d).start())
    arrived_sums[me, sub] = send_sums[me, sub]

    def mask(slot):
        @pl.loop(0, blocks)
        def _(k):
            gathered = jnp.zeros((WIDE, LANES), F32)
            for at in range(PAIR):
                p = k * PAIR + at
                row = row_full[slot, pl.ds(p, 1), :]
                full = jnp.where(col_full[slot] + row > 0.0, hgrad[slot, p], 0.0)
                gathered = gathered + full
                row_acc[slot, pl.ds(p, 1), :] = jnp.sum(full, axis=0, keepdims=True)
            col_acc[slot] += gathered

        def put_row(n):
            at = pl.ds(row_at(n), ext)
            feat_acc[at, :] += jnp.where(row_tiles[slot] == n, row_acc[slot], 0.0)

        def put_col(n):
            at = pl.ds(col_at(n), WIDE)
            feat_acc[at, :] += jnp.where(col_tiles[slot] == n, col_acc[slot], 0.0)

        each(0, bands, put_row)
        each(0, bands + 1, put_col)

    mask(0)
    for slot in range(1, slots):
        turn(slot)
        backward(slot)
        mask(slot)

    def feature(t):
        value = feat_acc[pl.ds(pl.multiple_of(RATE + t * rows, RATE), rows), :].astype(BF16)
        for half in range(2):
            send_feat[t, half] = value[half * half_rows : (half + 1) * half_rows]

    each(0, tiles, feature)

    def total_of(arrived):
        def add(t, carry):
            return carry + arrived[t, 0].astype(F32) + arrived[t, 1].astype(F32)

        return lax.fori_loop(0, tiles, add, jnp.zeros(arrived.shape[2:], F32))

    each(1, count, lambda d: scatter_of(d).wait())
    sums_out[me, sub] = total_of(arrived_sums).astype(BF16)
    each(1, count, lambda d: share_of(d).start())
    each(1, count, lambda d: feat_of(d).start())
    arrived_feat[me, sub] = send_feat[me, sub]

    @pl.loop(0, blocks)
    def _(k):
        for slot in range(slots):
            hidden = jnp.concatenate(
                [
                    jnp.concatenate(
                        [
                            part
                            for r in range(2)
                            for part in (
                                hid_even[slot, k * PAIR + r * RATE + i, 0:TILE],
                                hid_odd[slot, k * PAIR + r * RATE + i],
                                hid_even[slot, k * PAIR + r * RATE + i, PAIR:WIDE],
                            )
                        ],
                        axis=1,
                    )
                    for i in range(RATE)
                ],
                axis=0,
            )
            ahead = jnp.dot(hidden, weight_k[...], preferred_element_type=F32)
            for i in range(RATE):
                here = ahead[i * TILE : (i + 1) * TILE, LANES:] + kept[slot, i * TILE : (i + 1) * TILE, :]
                here = (here + bias_rows[slot, 0:1, :]).astype(BF16)
                turned = jnp.transpose(here, (1, 0)).astype(F32)
                lined[slot, (RATE + i) * out_channels : (RATE + i + 1) * out_channels, :] = turned[
                    0:out_channels
                ]
                lined[slot, i * out_channels : (i + 1) * out_channels, :] = turned[
                    HALF : HALF + out_channels
                ]
            kept[slot] = ahead[:, 0:LANES]
            at = pl.multiple_of(k * PAIR, PAIR)
            for o in range(out_channels):
                stage[slot, o, pl.ds(at, PAIR), :] = lined[
                    slot, pl.ds(o, PAIR, stride=out_channels), :
                ].astype(BF16)

    each(1, count, lambda d: feat_of(d).wait())
    feat_out[sub] = total_of(arrived_feat)
    handed = pltpu.make_async_remote_copy(
        src_ref=feat_out.at[sub], dst_ref=feat_out.at[sub],
        send_sem=pass_sem.at[0], recv_sem=pass_sem.at[1],
        device_id={"sub": 1 - sub}, device_id_type=MESH,
    )
    handed.start()
    each(1, count, lambda d: share_of(d).wait())
    handed.wait()


def finish_kernel(
    weight_rows, stage, feat_in, sums_in, pred_hbm, feat_ref, weight_ref, bias_ref, pred_sem
):
    sub_rows = pred_hbm.shape[2]
    copy = pltpu.make_async_copy(stage.at[:, :, pl.ds(PAIR, sub_rows), :], pred_hbm, pred_sem)
    copy.start()
    feat_ref[...] = feat_in[...].reshape(feat_ref.shape)
    sums = sums_in[...].astype(F32).reshape(-1, LANES)
    weight_ref[...] = sums[:weight_rows]
    bias_ref[...] = sums[weight_rows : weight_rows + 1, 0 : bias_ref.shape[1]]
    copy.wait()


def on_device(tiles, features, weight, out_bias, band_tiles, band_width, cotangent):
    rows, channels = features.shape
    slots, out_channels, sub_rows, _ = cotangent.shape
    total_bins = tiles * rows
    ext = sub_rows + PAIR
    blocks = ext // PAIR
    padded_rows = total_bins + WIDE
    weight_rows = 9 * out_channels
    chunk_rows = -(-(weight_rows + 16) // (2 * tiles * 16)) * 16
    vmem = pl.BlockSpec(memory_space=pltpu.VMEM)
    hbm = pl.BlockSpec(memory_space=pltpu.HBM)
    dma = pltpu.SemaphoreType.DMA
    shape = jax.ShapeDtypeStruct

    stage, feature_grad, sums = pl.pallas_call(
        functools.partial(fused_kernel, tiles),
        out_shape=(
            shape((slots, out_channels, ext, TILE), BF16),
            shape((2, rows // 2, channels), F32),
            shape((tiles, 2, chunk_rows, channels), BF16),
        ),
        in_specs=[hbm] * 6,
        out_specs=(vmem,) * 3,
        scratch_shapes=[
            pltpu.SMEM(band_tiles.shape, band_tiles.dtype),
            pltpu.SMEM(band_width.shape, band_width.dtype),
            pltpu.VMEM((1, out_channels), F32),
            pltpu.VMEM((tiles, rows, channels), BF16),
            pltpu.VMEM((padded_rows, channels), F32),
            pltpu.VMEM(cotangent.shape, BF16),
            pltpu.VMEM(weight.shape, BF16),
            pltpu.VMEM((12 * HALF, 2 * channels), BF16),
            pltpu.VMEM((6 * channels, 4 * HALF), BF16),
            pltpu.VMEM((out_channels * sub_rows, TILE), F32),
            pltpu.VMEM((slots, ext + PAIR, out_channels, TILE), BF16),
            pltpu.VMEM((blocks + 1, RATE, WIDE + PAIR, LANES), BF16),
            pltpu.VMEM((blocks + 1, RATE, WIDE, LANES), BF16),
            pltpu.VMEM((slots, ext, WIDE, channels), F32),
            pltpu.VMEM((slots, RATE, LANES), F32),
            pltpu.VMEM((slots, RATE, LANES), F32),
            pltpu.VMEM((slots, WIDE, channels), BF16),
            pltpu.VMEM((slots, TILE, channels), BF16),
            pltpu.VMEM((slots, WIDE, channels), F32),
            pltpu.VMEM((slots, ext, channels), F32),
            pltpu.VMEM((slots, ext, WIDE, channels), BF16),
            pltpu.VMEM((slots, ext, TILE, channels), BF16),
            pltpu.VMEM((4 * out_channels, 6 * channels), F32),
            pltpu.VMEM((slots, ext, channels), F32),
            pltpu.VMEM((slots, WIDE, channels), F32),
            pltpu.VMEM((padded_rows, channels), F32),
            pltpu.VMEM((slots, PAIR * out_channels, TILE), F32),
            pltpu.VMEM((slots, RATE * TILE, LANES), F32),
            pltpu.VMEM((tiles, 2, chunk_rows, channels), BF16),
            pltpu.VMEM((tiles, 2, chunk_rows, channels), BF16),
            pltpu.VMEM((tiles, 2, rows // 2, channels), BF16),
            pltpu.VMEM((tiles, 2, rows // 2, channels), BF16),
            dma((5,)),
            dma((slots,)),
            dma((2, tiles)),
            dma((2, 2 * tiles)),
            dma((2, 2 * tiles)),
            dma((2, 2 * tiles)),
            dma((2,)),
        ],
        compiler_params=pltpu.CompilerParams(
            collective_id=0, has_side_effects=True, vmem_limit_bytes=48 << 20
        ),
    )(
        *(
            pltpu.with_memory_space_constraint(x, pltpu.HBM)
            for x in (
                features, cotangent, weight, out_bias.reshape(1, out_channels), band_tiles, band_width
            )
        )
    )
    prediction, feature_grad, weight_grad, bias_grad = pl.pallas_call(
        functools.partial(finish_kernel, weight_rows),
        out_shape=(
            shape(cotangent.shape, BF16),
            shape((rows, channels), F32),
            shape((weight_rows, channels), F32),
            shape((1, out_channels), F32),
        ),
        in_specs=[vmem] * 3,
        out_specs=(hbm, vmem, vmem, vmem),
        scratch_shapes=[dma],
        compiler_params=pltpu.CompilerParams(vmem_limit_bytes=32 << 20),
    )(stage, feature_grad, sums)
    return (
        prediction,
        feature_grad,
        weight_grad.reshape(weight.shape),
        bias_grad.reshape(out_channels),
    )


def solution(mesh):
    in_specs = (
        P(("groups", "tile"), None),
        P(),
        P(),
        P(("groups", "tile")),
        P("groups"),
        P(("groups", "tile"), None, "sub", None),
    )
    out_specs = (
        P(("groups", "tile"), None, "sub", None),
        P(("groups", "tile"), None),
        P("groups", None, None, None),
        P("groups"),
    )
    return jax.shard_map(
        functools.partial(on_device, mesh.shape["tile"]),
        mesh=mesh, in_specs=in_specs, out_specs=out_specs, check_vma=False,
    )
```

```python
import functools

import jax
import jax.numpy as jnp
from jax import lax
from jax.experimental import pallas as pl
from jax.experimental.pallas import tpu as pltpu
from jax.sharding import PartitionSpec as P

RATE = 8
TILE = 128
BAND_T = 8
WIDE = TILE + 2 * RATE
PAIR = 2 * RATE
LANES = 128
HALF = 64
FAR = -1e30
MESH = pl.DeviceIdType.MESH
MARK = 2
F32 = jnp.float32
BF16 = jnp.bfloat16


def fused_kernel(
    tiles, x_hbm, cot_hbm, weight_hbm, bias_hbm, ids_hbm, width_hbm,
    stage, feat_out, sums_out,
    ids_ref, width_ref, out_bias_ref, held, feat_ref, cots, weights, stacked, weight_k,
    flat, cotp, even, odd, hgrad, bias_ref, bias_rows,
    col_even, col_odd, col_full, row_full, hid_even, hid_odd, weight_acc,
    row_acc, col_acc, feat_acc, lined, kept,
    send_sums, twin_sums, joined_sums, arrived_sums, send_feat, twin_feat, joined_feat, arrived_feat,
    table_sem, cot_sem, gather_sem, trade_sem, scatter_sem, share_sem, forward_sem, feat_sem,
):
    me = lax.axis_index("tile")
    sub = lax.axis_index("sub")
    count = 2 * tiles
    rows = x_hbm.shape[0]
    total = tiles * rows
    slots, out_channels, sub_rows, _ = cots.shape
    ext = sub_rows + PAIR
    blocks = ext // PAIR
    chunk_rows = send_sums.shape[2]
    other = 1 - sub
    twin = {"sub": other}
    half_rows = rows // 2

    def each(low, high, step):
        def body(d, carry):
            step(d)
            return carry

        lax.fori_loop(low, high, body, 0)

    def tile_of(d):
        return lax.rem(me + d, tiles)

    def remote(source, target, sems, d, where):
        return pltpu.make_async_remote_copy(
            src_ref=source, dst_ref=target, send_sem=sems.at[0, d], recv_sem=sems.at[1, d],
            device_id=where, device_id_type=MESH,
        )

    barrier = pltpu.get_barrier_semaphore()
    pl.semaphore_signal(barrier, inc=1, device_id={"sub": 1 - sub}, device_id_type=MESH)
    each(
        1, tiles,
        lambda d: pl.semaphore_signal(
            barrier, inc=1, device_id={"tile": tile_of(d)}, device_id_type=MESH
        ),
    )

    local = [
        pltpu.make_async_copy(source, target, table_sem.at[at])
        for at, (source, target) in enumerate(
            (
                (x_hbm, held.at[me]), (weight_hbm, weights), (bias_hbm, out_bias_ref),
                (ids_hbm, ids_ref), (width_hbm, width_ref),
            )
        )
    ]
    for copy in local:
        copy.start()

    def cot_copy(slot):
        return pltpu.make_async_copy(cot_hbm.at[slot], cots.at[slot], cot_sem.at[slot])

    for slot in range(slots):
        cot_copy(slot).start()

    feat_ref[0:RATE, :] = jnp.full((RATE, LANES), FAR, F32)
    tail = feat_ref.shape[0] - RATE - total
    feat_ref[RATE + total :, :] = jnp.full((tail, LANES), FAR, F32)
    for slab in (0, blocks):
        even[slab] = jnp.zeros(even.shape[1:], BF16)
        odd[slab] = jnp.zeros(odd.shape[1:], BF16)
    edge = jnp.zeros((blocks - 1, RATE, PAIR, LANES), BF16)
    even[1:blocks, :, 0:PAIR] = edge
    even[1:blocks, :, PAIR + TILE :] = edge
    stacked[...] = jnp.zeros_like(stacked)
    weight_acc[...] = jnp.zeros_like(weight_acc)
    feat_acc[...] = jnp.zeros_like(feat_acc)
    col_acc[...] = jnp.zeros_like(col_acc)
    kept[...] = jnp.zeros_like(kept)
    bias_rows[...] = jnp.zeros_like(bias_rows)
    for slot in range(slots):
        cotp[slot, 0:PAIR] = jnp.zeros((PAIR, out_channels, TILE), BF16)
        cotp[slot, PAIR + sub_rows :] = jnp.zeros((PAIR, out_channels, TILE), BF16)
    for copy in local:
        copy.wait()
    for j in range(4):
        for r in range(2):
            a = r + j - 1
            if 0 <= a <= 2:
                for b in range(3):
                    at = (b * 4 + j) * HALF
                    stacked[at : at + out_channels, r * LANES : (r + 1) * LANES] = weights[a, b]
    for b in range(3):
        for r in range(2):
            at = (r * 3 + b) * LANES
            weight_k[at : at + LANES, :] = jnp.transpose(
                stacked[b * 4 * HALF : (b + 1) * 4 * HALF, r * LANES : (r + 1) * LANES], (1, 0)
            )

    bands = total // TILE
    valids, row_tiles, col_tiles = [], [], []
    for slot in range(slots):
        tile_id = ids_ref[slot]
        tile_row = tile_id // BAND_T

        def width_at(n, width, tile_row=tile_row):
            return jnp.where(tile_row == n, width_ref[n], width)

        width = lax.fori_loop(0, bands, width_at, jnp.int32(0))
        offset = tile_id - tile_row * BAND_T
        valids.append(offset < width)
        row_tiles.append(jnp.where(valids[slot], tile_row, -1))
        col_tiles.append(jnp.where(valids[slot], tile_row + offset, -1))
        value = jnp.where(valids[slot], out_bias_ref[...], 0.0)
        bias_rows[slot, 0:1, 0:out_channels] = value
        bias_rows[slot, 0:1, HALF : HALF + out_channels] = value

    def arrange(slot):
        cot_copy(slot).wait()
        sums = []
        for o in range(out_channels):
            block = cots[slot, o].astype(F32)
            flat[o * sub_rows : (o + 1) * sub_rows, :] = block
            sums.append(jnp.sum(block, axis=0, keepdims=True))
        column = jnp.sum(jnp.transpose(jnp.concatenate(sums, axis=0), (1, 0)), axis=0, keepdims=True)
        bias_ref[slot] = jnp.zeros((RATE, LANES), F32)
        bias_ref[slot, 0:1, 0:out_channels] = column

        @pl.loop(0, sub_rows, unroll=16)
        def _(p):
            cotp[slot, PAIR + p] = flat[pl.ds(p, out_channels, stride=sub_rows), :].astype(BF16)

    def turn(slot):
        @pl.loop(0, blocks - 1)
        def _(k):
            low = jnp.zeros((HALF - out_channels, TILE), BF16)
            rim = jnp.zeros((RATE, LANES), F32)
            for i in range(RATE):
                at = PAIR + k * PAIR + i
                both = jnp.concatenate([cotp[slot, at + RATE], low, cotp[slot, at], low], axis=0)
                turned = jnp.transpose(both, (1, 0))
                even[k + 1, i, PAIR : PAIR + TILE] = turned
                odd[k + 1, i] = jnp.concatenate([rim, turned.astype(F32), rim], axis=0).astype(BF16)

    def backward(slot):
        @pl.loop(0, blocks)
        def _(k):
            left = jnp.concatenate(
                [
                    jnp.concatenate(
                        [
                            even[k + 1, i, PAIR:], even[k, i, PAIR:],
                            odd[k + 1, i], odd[k, i],
                            even[k + 1, i, 0:WIDE], even[k, i, 0:WIDE],
                        ],
                        axis=1,
                    )
                    for i in range(RATE)
                ],
                axis=0,
            )
            back = jnp.dot(left, stacked[...], preferred_element_type=F32)
            for i in range(RATE):
                for r in range(2):
                    p = k * PAIR + r * RATE + i
                    hgrad[slot, p] = back[i * WIDE : (i + 1) * WIDE, r * LANES : (r + 1) * LANES]

    def gather_of(d):
        return remote(held.at[me], held.at[me], gather_sem, d, {"tile": tile_of(d)})

    arrange(0)
    pl.semaphore_wait(barrier, tiles)
    each(1, tiles, lambda d: gather_of(d).start())
    at = pl.multiple_of(RATE + me * rows, RATE)
    feat_ref[pl.ds(at, rows), :] = held[me].astype(F32)
    for slot in range(1, slots):
        arrange(slot)
    turn(0)
    backward(0)

    def arrive(d):
        gather_of(d).wait()
        source = lax.rem(me - d + tiles, tiles)
        to = pl.multiple_of(RATE + source * rows, RATE)
        feat_ref[pl.ds(to, rows), :] = held[source].astype(F32)

    each(1, tiles, arrive)

    def row_at(n):
        return pl.multiple_of(n * TILE + sub * sub_rows, RATE)

    def col_at(n):
        return pl.multiple_of(n * TILE, TILE)

    for slot in range(slots):

        def take_row(n, held_rows, slot=slot):
            return jnp.where(row_tiles[slot] == n, feat_ref[pl.ds(row_at(n), ext), :], held_rows)

        def take_col(n, held_cols, slot=slot):
            return jnp.where(col_tiles[slot] == n, feat_ref[pl.ds(col_at(n), WIDE), :], held_cols)

        row_full[slot] = lax.fori_loop(0, bands, take_row, jnp.full((ext, LANES), FAR, F32))
        cols = lax.fori_loop(0, bands + 1, take_col, jnp.full((WIDE, LANES), FAR, F32))
        col_full[slot] = cols
        col_even[slot] = cols.astype(BF16)
        col_odd[slot] = cols[RATE : RATE + TILE].astype(BF16)

    def source_of(d):
        return lax.rem(me - d + tiles, tiles)

    def scatter_of(d):
        return remote(joined_sums.at[tile_of(d)], arrived_sums.at[d], scatter_sem, d, {"tile": tile_of(d)})

    def share_of(d):
        return remote(sums_out.at[sub, me], sums_out.at[sub, me], share_sem, d, {"tile": tile_of(d)})

    def forward_of(d):
        at = source_of(d)
        return remote(sums_out.at[sub, at], sums_out.at[sub, at], forward_sem, d, twin)

    def feat_of(d):
        return remote(joined_feat.at[tile_of(d)], arrived_feat.at[d], feat_sem, d, {"tile": tile_of(d)})

    trade_sums = remote(send_sums.at[other], twin_sums, trade_sem, 0, twin)
    trade_feat = remote(send_feat.at[other], twin_feat, trade_sem, 1, twin)
    handed = remote(feat_out.at[sub], feat_out.at[sub], trade_sem, 2, twin)

    def join(sent, got, joined):
        @pl.loop(0, tiles)
        def _(t):
            joined[t] = (sent[sub, t] + got[t]).astype(BF16)

    def total_of(joined, arrived):
        def add(d, carry):
            return carry + arrived[d].astype(F32)

        return lax.fori_loop(1, tiles, add, joined[me].astype(F32))

    def tap_of(slot, p, b):
        if b == 1:
            return hid_odd[slot, p]
        return hid_even[slot, p, 0:TILE] if b == 0 else hid_even[slot, p, PAIR:WIDE]

    for k in range(blocks):
        zero = jnp.zeros((), BF16)
        right, left = [], []
        for slot in range(slots):
            base_even = col_even[slot].reshape(WIDE // PAIR, PAIR, LANES)
            base_odd = col_odd[slot].reshape(TILE // PAIR, PAIR, LANES)
            for i in range(RATE):
                taps = []
                for r in range(2):
                    p = k * PAIR + r * RATE + i
                    row = row_full[slot, p : p + 1, :]
                    wide = jnp.broadcast_to(row, (PAIR, LANES)).astype(BF16)[None]
                    pair_even = jnp.maximum(base_even + wide, zero).reshape(WIDE, LANES)
                    pair_odd = jnp.maximum(base_odd + wide, zero).reshape(TILE, LANES)
                    hid_even[slot, p] = pair_even
                    hid_odd[slot, p] = pair_odd
                    taps += [pair_even[0:TILE], pair_odd, pair_even[PAIR:WIDE]]
                right.append(jnp.concatenate(taps, axis=1))
                left.append(
                    jnp.concatenate(
                        [cotp[slot, PAIR + k * PAIR + i + RATE * (1 - j)] for j in range(4)], axis=0
                    )
                )
        weight_acc[...] += jnp.dot(
            jnp.concatenate(left, axis=1), jnp.concatenate(right, axis=0), preferred_element_type=F32
        )

    def granule(row, value):
        at = row % chunk_rows
        chunk = row // chunk_rows
        send_sums[chunk // tiles, chunk % tiles, at : at + 16, :] = value

    row = 0
    for a in range(3):
        for b in range(3):
            full = (
                weight_acc[(a + 1) * out_channels : (a + 2) * out_channels, b * LANES : (b + 1) * LANES]
                + weight_acc[a * out_channels : (a + 1) * out_channels, (3 + b) * LANES : (4 + b) * LANES]
            )
            for at in range(0, out_channels, 16):
                granule(row, full[at : at + 16])
                row += 16
    bias_sum = jnp.zeros((RATE, LANES), F32)
    for slot in range(slots):
        bias_sum = bias_sum + jnp.where(valids[slot], bias_ref[slot], 0.0)
    granule(row, jnp.concatenate([bias_sum, jnp.zeros_like(bias_sum)], axis=0))
    row += 16
    while row % chunk_rows:
        granule(row, jnp.zeros((16, LANES), F32))
        row += 16

    def rest(c):
        send_sums[c // tiles, lax.rem(c, tiles)] = jnp.zeros((chunk_rows, LANES), F32)

    each(row // chunk_rows, count, rest)
    trade_sums.start()

    def mask(slot):
        @pl.loop(0, blocks)
        def _(k):
            gathered = jnp.zeros((WIDE, LANES), F32)
            for at in range(PAIR):
                p = k * PAIR + at
                row = row_full[slot, pl.ds(p, 1), :]
                full = jnp.where(col_full[slot] + row > 0.0, hgrad[slot, p], 0.0)
                gathered = gathered + full
                row_acc[slot, pl.ds(p, 1), :] = jnp.sum(full, axis=0, keepdims=True)
            col_acc[slot] += gathered

        def put_row(n):
            at = pl.ds(row_at(n), ext)
            feat_acc[at, :] += jnp.where(row_tiles[slot] == n, row_acc[slot], 0.0)

        def put_col(n):
            at = pl.ds(col_at(n), WIDE)
            feat_acc[at, :] += jnp.where(col_tiles[slot] == n, col_acc[slot], 0.0)

        each(0, bands, put_row)
        each(0, bands + 1, put_col)

    mask(0)
    trade_sums.wait()
    join(send_sums, twin_sums, joined_sums)
    each(1, tiles, lambda d: scatter_of(d).start())
    for slot in range(1, slots):
        turn(slot)
        backward(slot)
        mask(slot)

    def feature(t):
        value = feat_acc[pl.ds(pl.multiple_of(RATE + t * rows, RATE), rows), :]
        for half in range(2):
            send_feat[half, t] = value[half * half_rows : (half + 1) * half_rows]

    each(0, tiles, feature)

    trade_feat.start()
    each(1, tiles, lambda d: scatter_of(d).wait())
    sums_out[sub, me] = total_of(joined_sums, arrived_sums).astype(BF16)
    each(1, tiles, lambda d: share_of(d).start())
    forward_of(0).start()
    trade_feat.wait()
    join(send_feat, twin_feat, joined_feat)
    each(1, tiles, lambda d: feat_of(d).start())

    @pl.loop(0, blocks)
    def _(k):
        @pl.when(k == blocks - MARK)
        def _():
            def pass_on(d):
                share_of(d).wait()
                forward_of(d).start()

            each(1, tiles, pass_on)
            each(1, tiles, lambda d: feat_of(d).wait())
            feat_out[sub] = total_of(joined_feat, arrived_feat)
            handed.start()

        for slot in range(slots):
            hidden = jnp.concatenate(
                [
                    jnp.concatenate(
                        [
                            part
                            for r in range(2)
                            for part in [tap_of(slot, k * PAIR + r * RATE + i, b) for b in range(3)]
                        ],
                        axis=1,
                    )
                    for i in range(RATE)
                ],
                axis=0,
            )
            ahead = jnp.dot(hidden, weight_k[...], preferred_element_type=F32)
            for i in range(RATE):
                here = ahead[i * TILE : (i + 1) * TILE, LANES:] + kept[slot, i * TILE : (i + 1) * TILE, :]
                here = (here + bias_rows[slot, 0:1, :]).astype(BF16)
                turned = jnp.transpose(here, (1, 0)).astype(F32)
                lined[slot, (RATE + i) * out_channels : (RATE + i + 1) * out_channels, :] = turned[
                    0:out_channels
                ]
                lined[slot, i * out_channels : (i + 1) * out_channels, :] = turned[
                    HALF : HALF + out_channels
                ]
            kept[slot] = ahead[:, 0:LANES]
            at = pl.multiple_of(k * PAIR, PAIR)
            for o in range(out_channels):
                stage[slot, o, pl.ds(at, PAIR), :] = lined[
                    slot, pl.ds(o, PAIR, stride=out_channels), :
                ].astype(BF16)

    each(0, tiles, lambda d: forward_of(d).wait())
    handed.wait()


def finish_kernel(
    stage, feat_in, sums_in, pred_hbm, feat_hbm, weight_hbm, bias_hbm,
    feats, weights, bias, sems,
):
    slots, out_channels, sub_rows, _ = pred_hbm.shape
    copies = [
        pltpu.make_async_copy(
            stage.at[slot, pl.ds(half * (out_channels // 2), out_channels // 2), pl.ds(PAIR, sub_rows), :],
            pred_hbm.at[slot, pl.ds(half * (out_channels // 2), out_channels // 2)],
            sems.at[3 + slot * 2 + half],
        )
        for slot in range(slots)
        for half in range(2)
    ]
    for copy in copies:
        copy.start()
    sums = sums_in[...].astype(F32).reshape(-1, LANES)
    weights[...] = sums[0 : weights.shape[0]]
    bias[...] = sums[weights.shape[0] : weights.shape[0] + 1, 0:out_channels]
    feats[...] = feat_in[...].reshape(feats.shape)
    for at, (source, target) in enumerate(((weights, weight_hbm), (bias, bias_hbm), (feats, feat_hbm))):
        copies.append(pltpu.make_async_copy(source, target, sems.at[at]))
        copies[-1].start()
    for copy in copies:
        copy.wait()


def on_device(tiles, features, weight, out_bias, band_tiles, band_width, cotangent):
    rows, channels = features.shape
    slots, out_channels, sub_rows, _ = cotangent.shape
    total_bins = tiles * rows
    ext = sub_rows + PAIR
    blocks = ext // PAIR
    padded_rows = total_bins + WIDE
    weight_rows = 9 * out_channels
    chunk_rows = -(-(weight_rows + 16) // (2 * tiles * 16)) * 16
    vmem = pl.BlockSpec(memory_space=pltpu.VMEM)
    hbm = pl.BlockSpec(memory_space=pltpu.HBM)
    dma = pltpu.SemaphoreType.DMA
    shape = jax.ShapeDtypeStruct

    stage, feature_grad, sums = pl.pallas_call(
        functools.partial(fused_kernel, tiles),
        out_shape=(
            shape((slots, out_channels, ext, TILE), BF16),
            shape((2, rows // 2, channels), F32),
            shape((2, tiles, chunk_rows, channels), BF16),
        ),
        in_specs=[hbm] * 6,
        out_specs=(vmem,) * 3,
        scratch_shapes=[
            pltpu.SMEM(band_tiles.shape, band_tiles.dtype),
            pltpu.SMEM(band_width.shape, band_width.dtype),
            pltpu.VMEM((1, out_channels), F32),
            pltpu.VMEM((tiles, rows, channels), BF16),
            pltpu.VMEM((padded_rows, channels), F32),
            pltpu.VMEM(cotangent.shape, BF16),
            pltpu.VMEM(weight.shape, BF16),
            pltpu.VMEM((12 * HALF, 2 * channels), BF16),
            pltpu.VMEM((6 * channels, 4 * HALF), BF16),
            pltpu.VMEM((out_channels * sub_rows, TILE), F32),
            pltpu.VMEM((slots, ext + PAIR, out_channels, TILE), BF16),
            pltpu.VMEM((blocks + 1, RATE, WIDE + PAIR, LANES), BF16),
            pltpu.VMEM((blocks + 1, RATE, WIDE, LANES), BF16),
            pltpu.VMEM((slots, ext, WIDE, channels), F32),
            pltpu.VMEM((slots, RATE, LANES), F32),
            pltpu.VMEM((slots, RATE, LANES), F32),
            pltpu.VMEM((slots, WIDE, channels), BF16),
            pltpu.VMEM((slots, TILE, channels), BF16),
            pltpu.VMEM((slots, WIDE, channels), F32),
            pltpu.VMEM((slots, ext, channels), F32),
            pltpu.VMEM((slots, ext, WIDE, channels), BF16),
            pltpu.VMEM((slots, ext, TILE, channels), BF16),
            pltpu.VMEM((4 * out_channels, 6 * channels), F32),
            pltpu.VMEM((slots, ext, channels), F32),
            pltpu.VMEM((slots, WIDE, channels), F32),
            pltpu.VMEM((padded_rows, channels), F32),
            pltpu.VMEM((slots, PAIR * out_channels, TILE), F32),
            pltpu.VMEM((slots, RATE * TILE, LANES), F32),
            pltpu.VMEM((2, tiles, chunk_rows, channels), F32),
            pltpu.VMEM((tiles, chunk_rows, channels), F32),
            pltpu.VMEM((tiles, chunk_rows, channels), BF16),
            pltpu.VMEM((tiles, chunk_rows, channels), BF16),
            pltpu.VMEM((2, tiles, rows // 2, channels), F32),
            pltpu.VMEM((tiles, rows // 2, channels), F32),
            pltpu.VMEM((tiles, rows // 2, channels), BF16),
            pltpu.VMEM((tiles, rows // 2, channels), BF16),
            dma((5,)),
            dma((slots,)),
            dma((2, tiles)),
            dma((2, 3)),
            dma((2, tiles)),
            dma((2, tiles)),
            dma((2, tiles)),
            dma((2, tiles)),
        ],
        compiler_params=pltpu.CompilerParams(
            collective_id=0, has_side_effects=True, vmem_limit_bytes=50 << 20
        ),
    )(
        *(
            pltpu.with_memory_space_constraint(x, pltpu.HBM)
            for x in (
                features, cotangent, weight, out_bias.reshape(1, out_channels), band_tiles, band_width
            )
        )
    )
    prediction, feature_grad, weight_grad, bias_grad = pl.pallas_call(
        finish_kernel,
        out_shape=(
            shape(cotangent.shape, BF16),
            shape((rows, channels), F32),
            shape((weight_rows, channels), F32),
            shape((1, out_channels), F32),
        ),
        in_specs=[vmem] * 3,
        out_specs=(hbm,) * 4,
        scratch_shapes=[
            pltpu.VMEM((rows, channels), F32),
            pltpu.VMEM((weight_rows, channels), F32),
            pltpu.VMEM((1, out_channels), F32),
            dma((3 + 2 * slots,)),
        ],
        compiler_params=pltpu.CompilerParams(vmem_limit_bytes=32 << 20),
    )(stage, feature_grad, sums)
    return (
        prediction,
        feature_grad,
        weight_grad.reshape(weight.shape),
        bias_grad.reshape(out_channels),
    )


def solution(mesh):
    in_specs = (
        P(("groups", "tile"), None),
        P(),
        P(),
        P(("groups", "tile")),
        P("groups"),
        P(("groups", "tile"), None, "sub", None),
    )
    out_specs = (
        P(("groups", "tile"), None, "sub", None),
        P(("groups", "tile"), None),
        P("groups", None, None, None),
        P("groups"),
    )
    return jax.shard_map(
        functools.partial(on_device, mesh.shape["tile"]),
        mesh=mesh, in_specs=in_specs, out_specs=out_specs, check_vma=False,
    )
```

```python
import functools

import jax
import jax.numpy as jnp
from jax import lax
from jax.experimental import pallas as pl
from jax.experimental.pallas import tpu as pltpu
from jax.sharding import PartitionSpec as P

RATE = 8
TILE = 128
BAND_T = 8
WIDE = TILE + 2 * RATE
PAIR = 2 * RATE
LANES = 128
HALF = 64
FAR = -1e30
MESH = pl.DeviceIdType.MESH
MARK = 2
F32 = jnp.float32
BF16 = jnp.bfloat16


def fused_kernel(
    tiles, x_hbm, cot_hbm, weight_hbm, bias_hbm, ids_hbm, width_hbm,
    stage, feat_out, sums_out,
    ids_ref, width_ref, out_bias_ref, held, feat_ref, cots, weights, stacked, weight_k,
    flat, cotp, even, odd, hgrad, bias_ref, bias_rows,
    col_even, col_odd, col_full, row_full, hid_even, hid_odd, weight_acc,
    row_acc, col_acc, feat_acc, lined, kept,
    send_sums, twin_sums, joined_sums, arrived_sums, send_feat, twin_feat, joined_feat, arrived_feat,
    table_sem, cot_sem, gather_sem, trade_sem, scatter_sem, share_sem, forward_sem, feat_sem,
):
    me = lax.axis_index("tile")
    sub = lax.axis_index("sub")
    count = 2 * tiles
    rows = x_hbm.shape[0]
    total = tiles * rows
    slots, out_channels, sub_rows, _ = cots.shape
    ext = sub_rows + PAIR
    blocks = ext // PAIR
    chunk_rows = send_sums.shape[2]
    other = 1 - sub
    twin = {"sub": other}
    half_rows = rows // 2

    def each(low, high, step):
        def body(d, carry):
            step(d)
            return carry

        lax.fori_loop(low, high, body, 0)

    def tile_of(d):
        return lax.rem(me + d, tiles)

    def remote(source, target, sems, d, where):
        return pltpu.make_async_remote_copy(
            src_ref=source, dst_ref=target, send_sem=sems.at[0, d], recv_sem=sems.at[1, d],
            device_id=where, device_id_type=MESH,
        )

    barrier = pltpu.get_barrier_semaphore()
    pl.semaphore_signal(barrier, inc=1, device_id={"sub": 1 - sub}, device_id_type=MESH)
    each(
        1, tiles,
        lambda d: pl.semaphore_signal(
            barrier, inc=1, device_id={"tile": tile_of(d)}, device_id_type=MESH
        ),
    )

    local = [
        pltpu.make_async_copy(source, target, table_sem.at[at])
        for at, (source, target) in enumerate(
            (
                (x_hbm, held.at[me]), (weight_hbm, weights), (bias_hbm, out_bias_ref),
                (ids_hbm, ids_ref), (width_hbm, width_ref),
            )
        )
    ]
    for copy in local:
        copy.start()

    def cot_copy(slot):
        return pltpu.make_async_copy(cot_hbm.at[slot], cots.at[slot], cot_sem.at[slot])

    for slot in range(slots):
        cot_copy(slot).start()

    feat_ref[0:RATE, :] = jnp.full((RATE, LANES), FAR, F32)
    tail = feat_ref.shape[0] - RATE - total
    feat_ref[RATE + total :, :] = jnp.full((tail, LANES), FAR, F32)
    for slab in (0, blocks):
        even[slab] = jnp.zeros(even.shape[1:], BF16)
        odd[slab] = jnp.zeros(odd.shape[1:], BF16)
    edge = jnp.zeros((blocks - 1, RATE, PAIR, LANES), BF16)
    even[1:blocks, :, 0:PAIR] = edge
    even[1:blocks, :, PAIR + TILE :] = edge
    stacked[...] = jnp.zeros_like(stacked)
    weight_acc[...] = jnp.zeros_like(weight_acc)
    feat_acc[...] = jnp.zeros_like(feat_acc)
    col_acc[...] = jnp.zeros_like(col_acc)
    kept[...] = jnp.zeros_like(kept)
    bias_rows[...] = jnp.zeros_like(bias_rows)
    for slot in range(slots):
        cotp[slot, 0:PAIR] = jnp.zeros((PAIR, out_channels, TILE), BF16)
        cotp[slot, PAIR + sub_rows :] = jnp.zeros((PAIR, out_channels, TILE), BF16)
    for copy in local:
        copy.wait()
    for j in range(4):
        for r in range(2):
            a = r + j - 1
            if 0 <= a <= 2:
                for b in range(3):
                    at = (b * 4 + j) * HALF
                    stacked[at : at + out_channels, r * LANES : (r + 1) * LANES] = weights[a, b]
    for b in range(3):
        for r in range(2):
            at = (r * 3 + b) * LANES
            weight_k[at : at + LANES, :] = jnp.transpose(
                stacked[b * 4 * HALF : (b + 1) * 4 * HALF, r * LANES : (r + 1) * LANES], (1, 0)
            )

    bands = total // TILE
    valids, row_tiles, col_tiles = [], [], []
    for slot in range(slots):
        tile_id = ids_ref[slot]
        tile_row = tile_id // BAND_T

        def width_at(n, width, tile_row=tile_row):
            return jnp.where(tile_row == n, width_ref[n], width)

        width = lax.fori_loop(0, bands, width_at, jnp.int32(0))
        offset = tile_id - tile_row * BAND_T
        valids.append(offset < width)
        row_tiles.append(jnp.where(valids[slot], tile_row, -1))
        col_tiles.append(jnp.where(valids[slot], tile_row + offset, -1))
        value = jnp.where(valids[slot], out_bias_ref[...], 0.0)
        bias_rows[slot, 0:1, 0:out_channels] = value
        bias_rows[slot, 0:1, HALF : HALF + out_channels] = value

    def arrange(slot):
        cot_copy(slot).wait()
        sums = []
        for o in range(out_channels):
            block = cots[slot, o].astype(F32)
            flat[o * sub_rows : (o + 1) * sub_rows, :] = block
            sums.append(jnp.sum(block, axis=0, keepdims=True))
        column = jnp.sum(jnp.transpose(jnp.concatenate(sums, axis=0), (1, 0)), axis=0, keepdims=True)
        bias_ref[slot] = jnp.zeros((RATE, LANES), F32)
        bias_ref[slot, 0:1, 0:out_channels] = column

        @pl.loop(0, sub_rows, unroll=16)
        def _(p):
            cotp[slot, PAIR + p] = flat[pl.ds(p, out_channels, stride=sub_rows), :].astype(BF16)

    def turn(slot):
        @pl.loop(0, blocks - 1)
        def _(k):
            low = jnp.zeros((HALF - out_channels, TILE), BF16)
            rim = jnp.zeros((RATE, LANES), F32)
            for i in range(RATE):
                at = PAIR + k * PAIR + i
                both = jnp.concatenate([cotp[slot, at + RATE], low, cotp[slot, at], low], axis=0)
                turned = jnp.transpose(both, (1, 0))
                even[k + 1, i, PAIR : PAIR + TILE] = turned
                odd[k + 1, i] = jnp.concatenate([rim, turned.astype(F32), rim], axis=0).astype(BF16)

    def backward(slot, masked=False):
        @pl.loop(0, blocks)
        def _(k):
            left = jnp.concatenate(
                [
                    jnp.concatenate(
                        [
                            even[k + 1, i, PAIR:], even[k, i, PAIR:],
                            odd[k + 1, i], odd[k, i],
                            even[k + 1, i, 0:WIDE], even[k, i, 0:WIDE],
                        ],
                        axis=1,
                    )
                    for i in range(RATE)
                ],
                axis=0,
            )
            back = jnp.dot(left, stacked[...], preferred_element_type=F32)
            gathered = jnp.zeros((WIDE, LANES), F32)
            for i in range(RATE):
                for r in range(2):
                    p = k * PAIR + r * RATE + i
                    value = back[i * WIDE : (i + 1) * WIDE, r * LANES : (r + 1) * LANES]
                    if not masked:
                        hgrad[slot, p] = value
                        continue
                    row = row_full[slot, pl.ds(p, 1), :]
                    full = jnp.where(col_full[slot] + row > 0.0, value, 0.0)
                    gathered = gathered + full
                    row_acc[slot, pl.ds(p, 1), :] = jnp.sum(full, axis=0, keepdims=True)
            if masked:
                col_acc[slot] += gathered

    def gather_of(d):
        return remote(held.at[me], held.at[me], gather_sem, d, {"tile": tile_of(d)})

    arrange(0)
    pl.semaphore_wait(barrier, tiles)
    each(1, tiles, lambda d: gather_of(d).start())
    at = pl.multiple_of(RATE + me * rows, RATE)
    feat_ref[pl.ds(at, rows), :] = held[me].astype(F32)
    for slot in range(1, slots):
        arrange(slot)
    turn(0)
    backward(0)

    def arrive(d):
        gather_of(d).wait()
        source = lax.rem(me - d + tiles, tiles)
        to = pl.multiple_of(RATE + source * rows, RATE)
        feat_ref[pl.ds(to, rows), :] = held[source].astype(F32)

    each(1, tiles, arrive)

    def row_at(n):
        return pl.multiple_of(n * TILE + sub * sub_rows, RATE)

    def col_at(n):
        return pl.multiple_of(n * TILE, TILE)

    for slot in range(slots):

        def take_row(n, held_rows, slot=slot):
            return jnp.where(row_tiles[slot] == n, feat_ref[pl.ds(row_at(n), ext), :], held_rows)

        def take_col(n, held_cols, slot=slot):
            return jnp.where(col_tiles[slot] == n, feat_ref[pl.ds(col_at(n), WIDE), :], held_cols)

        row_full[slot] = lax.fori_loop(0, bands, take_row, jnp.full((ext, LANES), FAR, F32))
        cols = lax.fori_loop(0, bands + 1, take_col, jnp.full((WIDE, LANES), FAR, F32))
        col_full[slot] = cols
        col_even[slot] = cols.astype(BF16)
        col_odd[slot] = cols[RATE : RATE + TILE].astype(BF16)

    def source_of(d):
        return lax.rem(me - d + tiles, tiles)

    def scatter_of(d):
        return remote(joined_sums.at[tile_of(d)], arrived_sums.at[d], scatter_sem, d, {"tile": tile_of(d)})

    def share_of(d):
        return remote(sums_out.at[sub, me], sums_out.at[sub, me], share_sem, d, {"tile": tile_of(d)})

    def forward_of(d):
        at = source_of(d)
        return remote(sums_out.at[sub, at], sums_out.at[sub, at], forward_sem, d, twin)

    def feat_of(d):
        return remote(joined_feat.at[tile_of(d)], arrived_feat.at[d], feat_sem, d, {"tile": tile_of(d)})

    trade_sums = remote(send_sums.at[other], twin_sums, trade_sem, 0, twin)
    trade_feat = remote(send_feat.at[other], twin_feat, trade_sem, 1, twin)
    handed = remote(feat_out.at[sub], feat_out.at[sub], trade_sem, 2, twin)

    def join(sent, got, joined):
        @pl.loop(0, tiles)
        def _(t):
            joined[t] = (sent[sub, t] + got[t]).astype(BF16)

    def total_of(joined, arrived):
        def add(d, carry):
            return carry + arrived[d].astype(F32)

        return lax.fori_loop(1, tiles, add, joined[me].astype(F32))

    def tap_of(slot, p, b):
        if b == 1:
            return hid_odd[slot, p]
        return hid_even[slot, p, 0:TILE] if b == 0 else hid_even[slot, p, PAIR:WIDE]

    for k in range(blocks):
        zero = jnp.zeros((), BF16)
        right, left = [], []
        for slot in range(slots):
            base_even = col_even[slot].reshape(WIDE // PAIR, PAIR, LANES)
            base_odd = col_odd[slot].reshape(TILE // PAIR, PAIR, LANES)
            for i in range(RATE):
                taps = []
                for r in range(2):
                    p = k * PAIR + r * RATE + i
                    row = row_full[slot, p : p + 1, :]
                    wide = jnp.broadcast_to(row, (PAIR, LANES)).astype(BF16)[None]
                    pair_even = jnp.maximum(base_even + wide, zero).reshape(WIDE, LANES)
                    pair_odd = jnp.maximum(base_odd + wide, zero).reshape(TILE, LANES)
                    hid_even[slot, p] = pair_even
                    hid_odd[slot, p] = pair_odd
                    taps += [pair_even[0:TILE], pair_odd, pair_even[PAIR:WIDE]]
                right.append(jnp.concatenate(taps, axis=1))
                left.append(
                    jnp.concatenate(
                        [cotp[slot, PAIR + k * PAIR + i + RATE * (1 - j)] for j in range(4)], axis=0
                    )
                )
        weight_acc[...] += jnp.dot(
            jnp.concatenate(left, axis=1), jnp.concatenate(right, axis=0), preferred_element_type=F32
        )

    def granule(row, value):
        at = row % chunk_rows
        chunk = row // chunk_rows
        send_sums[chunk // tiles, chunk % tiles, at : at + 16, :] = value

    row = 0
    for a in range(3):
        for b in range(3):
            full = (
                weight_acc[(a + 1) * out_channels : (a + 2) * out_channels, b * LANES : (b + 1) * LANES]
                + weight_acc[a * out_channels : (a + 1) * out_channels, (3 + b) * LANES : (4 + b) * LANES]
            )
            for at in range(0, out_channels, 16):
                granule(row, full[at : at + 16])
                row += 16
    bias_sum = jnp.zeros((RATE, LANES), F32)
    for slot in range(slots):
        bias_sum = bias_sum + jnp.where(valids[slot], bias_ref[slot], 0.0)
    granule(row, jnp.concatenate([bias_sum, jnp.zeros_like(bias_sum)], axis=0))
    row += 16
    while row % chunk_rows:
        granule(row, jnp.zeros((16, LANES), F32))
        row += 16

    def rest(c):
        send_sums[c // tiles, lax.rem(c, tiles)] = jnp.zeros((chunk_rows, LANES), F32)

    each(row // chunk_rows, count, rest)
    trade_sums.start()

    def mask(slot):
        @pl.loop(0, blocks)
        def _(k):
            gathered = jnp.zeros((WIDE, LANES), F32)
            for at in range(PAIR):
                p = k * PAIR + at
                row = row_full[slot, pl.ds(p, 1), :]
                full = jnp.where(col_full[slot] + row > 0.0, hgrad[slot, p], 0.0)
                gathered = gathered + full
                row_acc[slot, pl.ds(p, 1), :] = jnp.sum(full, axis=0, keepdims=True)
            col_acc[slot] += gathered

        place(slot)

    def place(slot):
        def put_row(n):
            at = pl.ds(row_at(n), ext)
            feat_acc[at, :] += jnp.where(row_tiles[slot] == n, row_acc[slot], 0.0)

        def put_col(n):
            at = pl.ds(col_at(n), WIDE)
            feat_acc[at, :] += jnp.where(col_tiles[slot] == n, col_acc[slot], 0.0)

        each(0, bands, put_row)
        each(0, bands + 1, put_col)

    mask(0)
    trade_sums.wait()
    join(send_sums, twin_sums, joined_sums)
    each(1, tiles, lambda d: scatter_of(d).start())
    for slot in range(1, slots):
        turn(slot)
        backward(slot, masked=True)
        place(slot)

    def feature(t):
        value = feat_acc[pl.ds(pl.multiple_of(RATE + t * rows, RATE), rows), :]
        for half in range(2):
            send_feat[half, t] = value[half * half_rows : (half + 1) * half_rows]

    each(0, tiles, feature)

    trade_feat.start()
    each(1, tiles, lambda d: scatter_of(d).wait())
    sums_out[sub, me] = total_of(joined_sums, arrived_sums).astype(BF16)
    each(1, tiles, lambda d: share_of(d).start())
    forward_of(0).start()
    trade_feat.wait()
    join(send_feat, twin_feat, joined_feat)
    each(1, tiles, lambda d: feat_of(d).start())

    @pl.loop(0, blocks, unroll=blocks)
    def _(k):
        @pl.when(k == blocks - MARK)
        def _():
            def pass_on(d):
                share_of(d).wait()
                forward_of(d).start()

            each(1, tiles, pass_on)
            each(1, tiles, lambda d: feat_of(d).wait())
            feat_out[sub] = total_of(joined_feat, arrived_feat)
            handed.start()

        for slot in range(slots):
            hidden = jnp.concatenate(
                [
                    jnp.concatenate(
                        [
                            part
                            for r in range(2)
                            for part in [tap_of(slot, k * PAIR + r * RATE + i, b) for b in range(3)]
                        ],
                        axis=1,
                    )
                    for i in range(RATE)
                ],
                axis=0,
            )
            ahead = jnp.dot(hidden, weight_k[...], preferred_element_type=F32)
            for i in range(RATE):
                here = ahead[i * TILE : (i + 1) * TILE, LANES:] + kept[slot, i * TILE : (i + 1) * TILE, :]
                here = (here + bias_rows[slot, 0:1, :]).astype(BF16)
                turned = jnp.transpose(here, (1, 0)).astype(F32)
                lined[slot, (RATE + i) * out_channels : (RATE + i + 1) * out_channels, :] = turned[
                    0:out_channels
                ]
                lined[slot, i * out_channels : (i + 1) * out_channels, :] = turned[
                    HALF : HALF + out_channels
                ]
            kept[slot] = ahead[:, 0:LANES]
            at = pl.multiple_of(k * PAIR, PAIR)
            for o in range(out_channels):
                stage[slot, o, pl.ds(at, PAIR), :] = lined[
                    slot, pl.ds(o, PAIR, stride=out_channels), :
                ].astype(BF16)

    each(0, tiles, lambda d: forward_of(d).wait())
    handed.wait()


def finish_kernel(
    stage, feat_in, sums_in, pred_hbm, feat_hbm, weight_hbm, bias_hbm,
    feats, weights, bias, sems,
):
    slots, out_channels, sub_rows, _ = pred_hbm.shape
    copies = [
        pltpu.make_async_copy(
            stage.at[slot, pl.ds(half * (out_channels // 2), out_channels // 2), pl.ds(PAIR, sub_rows), :],
            pred_hbm.at[slot, pl.ds(half * (out_channels // 2), out_channels // 2)],
            sems.at[3 + slot * 2 + half],
        )
        for slot in range(slots)
        for half in range(2)
    ]
    for copy in copies:
        copy.start()
    sums = sums_in[...].astype(F32).reshape(-1, LANES)
    weights[...] = sums[0 : weights.shape[0]]
    bias[...] = sums[weights.shape[0] : weights.shape[0] + 1, 0:out_channels]
    feats[...] = feat_in[...].reshape(feats.shape)
    for at, (source, target) in enumerate(((weights, weight_hbm), (bias, bias_hbm), (feats, feat_hbm))):
        copies.append(pltpu.make_async_copy(source, target, sems.at[at]))
        copies[-1].start()
    for copy in copies:
        copy.wait()


def on_device(tiles, features, weight, out_bias, band_tiles, band_width, cotangent):
    rows, channels = features.shape
    slots, out_channels, sub_rows, _ = cotangent.shape
    total_bins = tiles * rows
    ext = sub_rows + PAIR
    blocks = ext // PAIR
    padded_rows = total_bins + WIDE
    weight_rows = 9 * out_channels
    chunk_rows = -(-(weight_rows + 16) // (2 * tiles * 16)) * 16
    vmem = pl.BlockSpec(memory_space=pltpu.VMEM)
    hbm = pl.BlockSpec(memory_space=pltpu.HBM)
    dma = pltpu.SemaphoreType.DMA
    shape = jax.ShapeDtypeStruct

    stage, feature_grad, sums = pl.pallas_call(
        functools.partial(fused_kernel, tiles),
        out_shape=(
            shape((slots, out_channels, ext, TILE), BF16),
            shape((2, rows // 2, channels), F32),
            shape((2, tiles, chunk_rows, channels), BF16),
        ),
        in_specs=[hbm] * 6,
        out_specs=(vmem,) * 3,
        scratch_shapes=[
            pltpu.SMEM(band_tiles.shape, band_tiles.dtype),
            pltpu.SMEM(band_width.shape, band_width.dtype),
            pltpu.VMEM((1, out_channels), F32),
            pltpu.VMEM((tiles, rows, channels), BF16),
            pltpu.VMEM((padded_rows, channels), F32),
            pltpu.VMEM(cotangent.shape, BF16),
            pltpu.VMEM(weight.shape, BF16),
            pltpu.VMEM((12 * HALF, 2 * channels), BF16),
            pltpu.VMEM((6 * channels, 4 * HALF), BF16),
            pltpu.VMEM((out_channels * sub_rows, TILE), F32),
            pltpu.VMEM((slots, ext + PAIR, out_channels, TILE), BF16),
            pltpu.VMEM((blocks + 1, RATE, WIDE + PAIR, LANES), BF16),
            pltpu.VMEM((blocks + 1, RATE, WIDE, LANES), BF16),
            pltpu.VMEM((slots, ext, WIDE, channels), F32),
            pltpu.VMEM((slots, RATE, LANES), F32),
            pltpu.VMEM((slots, RATE, LANES), F32),
            pltpu.VMEM((slots, WIDE, channels), BF16),
            pltpu.VMEM((slots, TILE, channels), BF16),
            pltpu.VMEM((slots, WIDE, channels), F32),
            pltpu.VMEM((slots, ext, channels), F32),
            pltpu.VMEM((slots, ext, WIDE, channels), BF16),
            pltpu.VMEM((slots, ext, TILE, channels), BF16),
            pltpu.VMEM((4 * out_channels, 6 * channels), F32),
            pltpu.VMEM((slots, ext, channels), F32),
            pltpu.VMEM((slots, WIDE, channels), F32),
            pltpu.VMEM((padded_rows, channels), F32),
            pltpu.VMEM((slots, PAIR * out_channels, TILE), F32),
            pltpu.VMEM((slots, RATE * TILE, LANES), F32),
            pltpu.VMEM((2, tiles, chunk_rows, channels), F32),
            pltpu.VMEM((tiles, chunk_rows, channels), F32),
            pltpu.VMEM((tiles, chunk_rows, channels), BF16),
            pltpu.VMEM((tiles, chunk_rows, channels), BF16),
            pltpu.VMEM((2, tiles, rows // 2, channels), F32),
            pltpu.VMEM((tiles, rows // 2, channels), F32),
            pltpu.VMEM((tiles, rows // 2, channels), BF16),
            pltpu.VMEM((tiles, rows // 2, channels), BF16),
            dma((5,)),
            dma((slots,)),
            dma((2, tiles)),
            dma((2, 3)),
            dma((2, tiles)),
            dma((2, tiles)),
            dma((2, tiles)),
            dma((2, tiles)),
        ],
        compiler_params=pltpu.CompilerParams(
            collective_id=0, has_side_effects=True, vmem_limit_bytes=50 << 20
        ),
    )(
        *(
            pltpu.with_memory_space_constraint(x, pltpu.HBM)
            for x in (
                features, cotangent, weight, out_bias.reshape(1, out_channels), band_tiles, band_width
            )
        )
    )
    prediction, feature_grad, weight_grad, bias_grad = pl.pallas_call(
        finish_kernel,
        out_shape=(
            shape(cotangent.shape, BF16),
            shape((rows, channels), F32),
            shape((weight_rows, channels), F32),
            shape((1, out_channels), F32),
        ),
        in_specs=[vmem] * 3,
        out_specs=(hbm,) * 4,
        scratch_shapes=[
            pltpu.VMEM((rows, channels), F32),
            pltpu.VMEM((weight_rows, channels), F32),
            pltpu.VMEM((1, out_channels), F32),
            dma((3 + 2 * slots,)),
        ],
        compiler_params=pltpu.CompilerParams(vmem_limit_bytes=32 << 20),
    )(stage, feature_grad, sums)
    return (
        prediction,
        feature_grad,
        weight_grad.reshape(weight.shape),
        bias_grad.reshape(out_channels),
    )


def solution(mesh):
    in_specs = (
        P(("groups", "tile"), None),
        P(),
        P(),
        P(("groups", "tile")),
        P("groups"),
        P(("groups", "tile"), None, "sub", None),
    )
    out_specs = (
        P(("groups", "tile"), None, "sub", None),
        P(("groups", "tile"), None),
        P("groups", None, None, None),
        P("groups"),
    )
    return jax.shard_map(
        functools.partial(on_device, mesh.shape["tile"]),
        mesh=mesh, in_specs=in_specs, out_specs=out_specs, check_vma=False,
    )
```
